128 devices in a mesh: area: 32 (over z, x, core), harm: 4 (over y).
Axes of the slice: x: 4, y: 4, z: 4, core: 2. Of those that a mesh axis runs over, the one named last changes fastest.
Arguments:
- volt: float32 [2, 32, 28, 32, 768], P(None, 'area', 'harm'), may hold values from -3 to 3
- inject: float32 [2, 32, 28, 32, 768], P(None, 'area', 'harm'), may hold values from -6 to 6
- zinv: bfloat16 [2, 32, 28, 768, 768], P(None, 'area', 'harm')
- dev_bus: int32 [32, 2048], P('area'), may hold values from 0 to 767
- dev_count: int32 [32], P('area'), may hold values from 1 to 2048, 32768 in all
- dev_cond: float32 [32, 2048], P('area'), may hold values from 0.1 to 1
- dev_sat: float32 [32, 2048], P('area'), may hold values from 0.2 to 2
- tie_bus: int32 [32, 256], P('area'), may hold values from 0 to 127
- tie_area: int32 [32, 256, 1], P('area'), may hold values from 0 to 31; in each aligned block of 256 rows (0 to 255, 256 to 511, ..., all dimensions but the last counted through in order) at most 16 rows name the same one
- tie_far: int32 [32, 256], P('area'), may hold values from 0 to 127
- tie_res: float32 [32, 256], P('area'), may hold values from 0.5 to 2
- tie_reac: float32 [32, 256], P('area'), may hold values from 0.01 to 0.1
Outputs:
- volt_next: float32 [2, 32, 28, 32, 768], P(None, 'area', 'harm')
The draws below stay inside these ranges and needn't reach their ends.
Inputs may be any that keep to these rules, and one draw needn't show every extreme that they name: `dev_count`: slot k of an area holds an inverter exactly when k is below its count; the counts sum to 32768 and some area has exactly 2048 inverters. `tie_area`: in one area's list no area is named more than 16 times, and in some list some area is named exactly 16 times; every area is named in some list; a list may name its own area.
All inputs are finite; a program needn't handle non-finite values. No bound on the sum of `dev_count` on one device may be relied on, other than what follows from the above.
Results may differ from the reference program's by a relative error of at most 0.0029.
Values sent between devices are 32-bit elements; how exact they have to be, the bound alone decides.
A program may use at most 128 MiB of HBM per device.

```python
import math
import jax
import jax.numpy as jnp
import numpy as np
from jax import lax

NB = 768
NBD = 128
H = 28
TS = 512
CAP = 2048
NT = 256
SCEN = 32
AREAS = 32
PEER_CAP = 16


def draw_zinv(key, part):
    key_noise, key_real, key_imag = jax.random.split(key, 3)
    shape = (2, AREAS, H, NB, NB)
    noise_part = jax.random.normal(key_noise, shape, jnp.float32)
    noise_part = noise_part * (0.5 / math.sqrt(NB))
    diag_real = jnp.exp(jax.random.uniform(key_real, (AREAS, H, NB), jnp.float32, math.log(0.5), math.log(2.0)))
    diag_imag = jax.random.uniform(key_imag, (AREAS, H, NB), jnp.float32, -0.5, 0.5)
    diagonal = jnp.stack([diag_real, diag_imag])[..., None]
    row_ids = lax.broadcasted_iota(jnp.int32, (NB, NB), 0)
    col_ids = lax.broadcasted_iota(jnp.int32, (NB, NB), 1)
    on_diagonal = row_ids == col_ids
    return (noise_part + jnp.where(on_diagonal, diagonal, 0.0)).astype(jnp.bfloat16)


def plant(values, key, low, high):
    extent = values.shape
    index_at = [jax.random.randint(jax.random.fold_in(key, axis), (), 0, extent[axis]) for axis in range(len(extent))]
    values = values.at[tuple(index_at)].set(low)
    longest = extent.index(max(extent))
    index_at[longest] = (index_at[longest] + 1) % extent[longest]
    return values.at[tuple(index_at)].set(high)


def shard_levels(key, shape, shards, least, high):
    def one(dim, shards_of):
        heights = jax.random.uniform(jax.random.fold_in(jax.random.fold_in(key, 6), dim), (shards_of,), jnp.float32, least / len(shards), high / len(shards))
        return jnp.repeat(jnp.exp(heights), shape[dim] // shards_of).reshape((-1,) + (1,) * (len(shape) - dim - 1))

    loudness = one(*shards[0])
    for cut in shards[1:]:
        loudness = loudness * one(*cut)
    return loudness


def split_up(number_of, total, most, lean):
    weights = [(1 << 20) // math.isqrt(standing ** lean) + 1 for standing in range(2, number_of + 1)]
    rest, holding = total - most - (number_of - 1), [1] * (number_of - 1)
    while rest > 0:
        movable = [i for i in range(number_of - 1) if holding[i] < most]
        mass, left = sum([weights[i] for i in movable]), rest
        for i in movable:
            extra = min(most - holding[i], max(1, left * weights[i] // mass), rest)
            holding[i] = holding[i] + extra
            rest = rest - extra
    return np.array([most] + holding)


def ragged(own_key, count, total, bound, slope):
    if count == 2:
        one = jax.random.randint(own_key, (), max(1, total - bound), min(bound, total - 1) + 1)
        return jnp.stack([one, total - one])
    lengths = jnp.asarray(split_up(count, total, bound, slope), jnp.int32)
    pairs = (count - 1) // 2
    giver, sink = lengths[1:1 + 2 * pairs:2], lengths[2:2 + 2 * pairs:2]
    margin = jnp.minimum(giver - 1, bound - sink)
    moved = jax.random.randint(jax.random.fold_in(own_key, 1), (pairs,), 0, 1 << 20) % (margin + 1)
    lengths = lengths.at[1:1 + 2 * pairs:2].set(giver - moved).at[2:2 + 2 * pairs:2].set(sink + moved)
    return lengths[jax.random.permutation(jax.random.fold_in(own_key, 2), count)]


def shared_out(stream_key, own, number, rows, count, top, limit, skew):
    ranking = jax.random.permutation(stream_key, count)
    packed, ordinary = shares(count, rows * top, limit, skew, True), shares(count, rows * top, limit, skew, False)
    places = jnp.arange(count)

    def named(sizes, turn):
        used = int((sizes > 0).sum())
        fixed = max(1, used // 4)
        shifted = fixed + (places - fixed + turn * (used - fixed)) % max(1, count - fixed)
        return jnp.zeros((count,), jnp.int32).at[ranking[jnp.where(places < fixed, places, shifted)]].set(jnp.asarray(sizes, jnp.int32))

    sizes = jnp.where(number % 4 == 0, named(packed, number // 4), named(ordinary, number - number // 4 - 1))
    mixed = jax.random.permutation(jax.random.fold_in(own, 3), count)
    source_of, taker = mixed[0:count // 2 * 2:2], mixed[1:count // 2 * 2:2]
    room = jnp.minimum(sizes[source_of] - 1, limit - sizes[taker]) // 2
    room = jnp.where((source_of == ranking[0]) | (taker == ranking[0]) | (sizes[taker] == 0), 0, jnp.maximum(room, 0))
    shifted = jax.random.randint(jax.random.fold_in(own, 4), (count // 2,), 0, 1 << 20) % (room + 1)
    sizes = sizes.at[source_of].add(-shifted).at[taker].add(shifted)
    labels = jnp.searchsorted(jnp.cumsum(sizes), jnp.arange(rows * top), side="right").astype(jnp.int32)
    listing = labels.reshape(top, rows).T
    listing = listing[jax.random.permutation(jax.random.fold_in(own, 1), rows)]
    turn = jax.random.randint(jax.random.fold_in(own, 2), (rows, 1), 0, top)
    return jnp.take_along_axis(listing, (jnp.arange(top)[None, :] + turn) % top, axis=1)


def shares(number_of, total, most, skew, full):
    loads = [(1 << 20) // math.isqrt(rank ** skew) + 1 for rank in range(1, number_of + 1)]
    largest = most if full else min(most, max(-(-total // number_of), total * loads[0] // sum(loads)))
    least = 1 if total - largest >= number_of - 1 else 0
    counts, surplus = [largest] + [least] * (number_of - 1), total - largest - least * (number_of - 1)
    while surplus > 0:
        candidates = [i for i in range(1, number_of) if counts[i] < largest] or [i for i in range(1, number_of) if counts[i] < most]
        whole, left = sum([loads[i] for i in candidates]), surplus
        for i in candidates:
            extra = min(most - counts[i], max(1, left * loads[i] // whole), surplus)
            counts[i] = counts[i] + extra
            surplus = surplus - extra
    return np.array(counts)


def bell_draw(rng, shape, scale, reach, shards=(), kind=jnp.bfloat16):
    level = shard_levels(rng, shape, shards, -0.22, 0.18) if shards else 1.0
    array = jax.random.normal(rng, shape, jnp.float32) * scale * level
    return jnp.minimum(jnp.maximum(array, -reach), reach).astype(kind)


def setup_inputs(seed: int = 0) -> dict:
    streams_of = jax.random.split(jax.random.key(seed), 13)
    volt = bell_draw(streams_of[0], (2, AREAS, H, SCEN, NB), 0.5, 3.0, ((1, 32), (2, 4)), jnp.float32)
    inject = bell_draw(streams_of[1], (2, AREAS, H, SCEN, NB), 1.0, 6.0, ((1, 32), (2, 4)), jnp.float32)
    zinv = draw_zinv(jax.random.fold_in(streams_of[12], 71), 0)
    dev_bus = plant(jax.random.randint(streams_of[3], (AREAS, CAP), 0, NB), jax.random.fold_in(streams_of[3], 1), 0, NB - 1).astype(jnp.int32)
    dev_count = ragged(streams_of[4], AREAS, AREAS * CAP // 2, CAP, 2).astype(jnp.int32)
    dev_cond = jnp.clip(jnp.exp(math.log(1.0) - 2.3025851 * jax.random.uniform(streams_of[5], (AREAS, CAP), jnp.float32) ** shard_levels(streams_of[5], (AREAS, CAP), ((0, 32),), -0.2, 0.2)), 0.1, 1.0)
    dev_sat = jnp.clip(jnp.exp(math.log(2.0) - 2.3025851 * jax.random.uniform(streams_of[6], (AREAS, CAP), jnp.float32) ** shard_levels(streams_of[6], (AREAS, CAP), ((0, 32),), -0.2, 0.2)), 0.2, 2.0)
    tie_bus = plant(jax.random.randint(streams_of[7], (AREAS, NT), 0, NBD), jax.random.fold_in(streams_of[7], 1), 0, NBD - 1).astype(jnp.int32)
    tie_area_keys = jax.random.split(jax.random.fold_in(streams_of[8], 1), AREAS * NT // NT)
    tie_area_turns = jax.random.permutation(jax.random.fold_in(streams_of[8], 3), AREAS * NT // NT)
    tie_area = jax.vmap(lambda own, number: shared_out(jax.random.fold_in(streams_of[8], 2), own, number, NT, AREAS, 1, PEER_CAP, 2))(tie_area_keys, tie_area_turns).reshape((AREAS, NT, 1))
    tie_far = plant(jax.random.randint(streams_of[9], (AREAS, NT), 0, NBD), jax.random.fold_in(streams_of[9], 1), 0, NBD - 1).astype(jnp.int32)
    tie_res = jnp.clip(jnp.exp(math.log(2.0) - 1.3862944 * jax.random.uniform(streams_of[10], (AREAS, NT), jnp.float32) ** shard_levels(streams_of[10], (AREAS, NT), ((0, 32),), -0.2, 0.2)), 0.5, 2.0)
    tie_reac = jnp.clip(jnp.exp(math.log(0.1) - 2.3025851 * jax.random.uniform(streams_of[11], (AREAS, NT), jnp.float32) ** shard_levels(streams_of[11], (AREAS, NT), ((0, 32),), -0.2, 0.2)), 0.01, 0.1)
    return {"volt": volt, "inject": inject, "zinv": zinv, "dev_bus": dev_bus, "dev_count": dev_count, "dev_cond": dev_cond, "dev_sat": dev_sat, "tie_bus": tie_bus, "tie_area": tie_area, "tie_far": tie_far, "tie_res": tie_res, "tie_reac": tie_reac}


HIGH = lax.Precision.HIGHEST


def phase_table(first_row, row_count):
    sample_ids = jnp.arange(TS, dtype=jnp.int32)[:, None]
    orders = 2 * (first_row + jnp.arange(row_count, dtype=jnp.int32)) + 1
    phase_turns = (sample_ids * orders[None, :]) % TS
    angles = phase_turns.astype(jnp.float32) * (2.0 * math.pi / TS)
    return jnp.cos(angles), jnp.sin(angles)


def reference(volt, inject, zinv, dev_bus, dev_count, dev_cond, dev_sat, tie_bus, tie_area, tie_far, tie_res, tie_reac):
    cosine_table, sine_table = phase_table(0, H)
    orders = (2 * jnp.arange(H, dtype=jnp.int32) + 1).astype(jnp.float32)
    bus_ids = jnp.arange(NB, dtype=jnp.int32)
    edge_ids = jnp.arange(NBD, dtype=jnp.int32)
    slot_ids = jnp.arange(CAP, dtype=jnp.int32)

    def one_area(area_index):
        volt_area = lax.dynamic_index_in_dim(volt, area_index, 1, keepdims=False)
        inject_area = lax.dynamic_index_in_dim(inject, area_index, 1, keepdims=False)
        zinv_area = lax.dynamic_index_in_dim(zinv, area_index, 1, keepdims=False).astype(jnp.float32)
        dev_buses = dev_bus[area_index]
        live_slot = (slot_ids < dev_count[area_index]).astype(jnp.float32)
        dev_volt = jnp.take(volt_area, dev_buses, axis=3)
        waveform = jnp.einsum("th,hsk->tsk", cosine_table, dev_volt[0], precision=HIGH) - jnp.einsum("th,hsk->tsk", sine_table, dev_volt[1], precision=HIGH)
        current = (dev_cond[area_index] * live_slot) * waveform + (dev_sat[area_index] * live_slot) * jnp.tanh(2.0 * waveform)
        harm_real = (2.0 / TS) * jnp.einsum("th,tsk->hsk", cosine_table, current, precision=HIGH)
        harm_imag = -(2.0 / TS) * jnp.einsum("th,tsk->hsk", sine_table, current, precision=HIGH)
        onehot = (dev_buses[:, None] == bus_ids[None, :]).astype(jnp.float32)
        bus_real = jnp.einsum("hsk,kb->hsb", harm_real, onehot, precision=HIGH)
        bus_imag = jnp.einsum("hsk,kb->hsb", harm_imag, onehot, precision=HIGH)
        targets = tie_area[area_index, :, 0]
        far_bus = tie_far[area_index]
        far_volt = volt[:, targets, :, :, far_bus]
        resist = tie_res[area_index][:, None]
        reactance = tie_reac[area_index][:, None] * orders[None, :]
        denominator = resist * resist + reactance * reactance
        adm_real = (resist / denominator)[:, :, None]
        adm_imag = (-reactance / denominator)[:, :, None]
        tie_real = adm_real * far_volt[:, 0] - adm_imag * far_volt[:, 1]
        tie_imag = adm_real * far_volt[:, 1] + adm_imag * far_volt[:, 0]
        tie_onehot = (tie_bus[area_index][:, None] == edge_ids[None, :]).astype(jnp.float32)
        tie_real_sum = jnp.einsum("ths,tb->hsb", tie_real, tie_onehot, precision=HIGH)
        tie_imag_sum = jnp.einsum("ths,tb->hsb", tie_imag, tie_onehot, precision=HIGH)
        padding = jnp.zeros((H, SCEN, NB - NBD), jnp.float32)
        rhs_real = (inject_area[0] + bus_real + jnp.concatenate([tie_real_sum, padding], axis=2)).astype(jnp.bfloat16)
        rhs_imag = (inject_area[1] + bus_imag + jnp.concatenate([tie_imag_sum, padding], axis=2)).astype(jnp.bfloat16)
        rhs_real = lax.optimization_barrier(rhs_real).astype(jnp.float32)
        rhs_imag = lax.optimization_barrier(rhs_imag).astype(jnp.float32)
        next_real = jnp.einsum("hij,hsj->hsi", zinv_area[0], rhs_real, precision=HIGH) - jnp.einsum("hij,hsj->hsi", zinv_area[1], rhs_imag, precision=HIGH)
        next_imag = jnp.einsum("hij,hsj->hsi", zinv_area[0], rhs_imag, precision=HIGH) + jnp.einsum("hij,hsj->hsi", zinv_area[1], rhs_real, precision=HIGH)
        return jnp.stack([next_real, next_imag])

    result = lax.map(one_area, jnp.arange(AREAS, dtype=jnp.int32))
    return jnp.moveaxis(result, 0, 1)
```

```python
import math

import jax
import jax.numpy as jnp
from jax import lax
from jax.sharding import PartitionSpec as P

NB = 768
NBD = 128
H = 28
TS = 512
HALF = TS // 2
CAP = 2048
SCEN = 32

HIGH = lax.Precision.HIGHEST


def phase_table():
    sample_ids = jnp.arange(HALF, dtype=jnp.int32)[:, None]
    orders = 2 * jnp.arange(H, dtype=jnp.int32) + 1
    phase_turns = sample_ids * orders[None, :] % TS
    angles = phase_turns.astype(jnp.float32) * (2.0 * math.pi / TS)
    return jnp.concatenate([jnp.cos(angles), -jnp.sin(angles)], axis=1)


def per_device(
    volt,
    inject,
    zinv,
    dev_bus,
    dev_count,
    dev_cond,
    dev_sat,
    tie_bus,
    tie_area,
    tie_far,
    tie_res,
    tie_reac,
):
    h_local = volt.shape[2]
    harm_index = lax.axis_index("harm")
    own = volt[:, 0]
    table = phase_table()
    spread = lax.all_to_all(own, "harm", 2, 1, tiled=True)
    s_local = spread.shape[2]
    spread = spread.reshape(2 * H, s_local, NB)
    waveform = jnp.einsum("tc,csb->tsb", table, spread, precision=HIGH)
    shape = jnp.tanh(2.0 * waveform)
    harmonics = (4.0 / TS) * jnp.einsum("tc,tsb->csb", table, shape, precision=HIGH)
    back = lax.all_to_all(
        harmonics.reshape(2, H, s_local, NB), "harm", 1, 2, tiled=True
    )
    live = (jnp.arange(CAP, dtype=jnp.int32) < dev_count[0]).astype(jnp.float32)
    onehot = (dev_bus[0][:, None] == jnp.arange(NB, dtype=jnp.int32)[None, :]).astype(
        jnp.float32
    )
    sums = jnp.einsum(
        "pk,kb->pb", jnp.stack([live * dev_cond[0], live * dev_sat[0]]), onehot, precision=HIGH
    )
    gathered = lax.all_gather(own[..., :NBD], "area", axis=3, tiled=True)
    entry = tie_area[0, :, 0] * NBD + tie_far[0]
    pick = (
        jnp.arange(gathered.shape[3], dtype=jnp.int32)[:, None] == entry[None, :]
    ).astype(jnp.float32)
    far_volt = jnp.einsum("chse,ej->chsj", gathered, pick, precision=HIGH)
    orders = (2 * (harm_index * h_local + jnp.arange(h_local, dtype=jnp.int32)) + 1).astype(
        jnp.float32
    )
    resist = tie_res[0][None, :]
    reactance = tie_reac[0][None, :] * orders[:, None]
    denominator = resist * resist + reactance * reactance
    adm_real = (resist / denominator)[:, None, :]
    adm_imag = (-reactance / denominator)[:, None, :]
    tie_onehot = (tie_bus[0][:, None] == jnp.arange(NBD, dtype=jnp.int32)[None, :]).astype(
        jnp.float32
    )
    tie = jnp.stack(
        [
            adm_real * far_volt[0] - adm_imag * far_volt[1],
            adm_real * far_volt[1] + adm_imag * far_volt[0],
        ]
    )
    tie_sum = jnp.einsum("chsj,jb->chsb", tie, tie_onehot, precision=HIGH)
    tie_sum = jnp.pad(tie_sum, ((0, 0), (0, 0), (0, 0), (0, NB - NBD)))
    rhs = (inject[:, 0] + sums[0] * own + sums[1] * back + tie_sum).astype(jnp.bfloat16)
    both = jnp.concatenate([rhs[0], rhs[1]], axis=1)
    turned = jnp.concatenate([-rhs[1], rhs[0]], axis=1)
    result = jnp.einsum(
        "hij,hsj->hsi", zinv[0, 0], both, preferred_element_type=jnp.float32
    ) + jnp.einsum("hij,hsj->hsi", zinv[1, 0], turned, preferred_element_type=jnp.float32)
    return jnp.stack([result[:, :SCEN], result[:, SCEN:]])[:, None]


def solution(mesh):
    in_specs = (
        P(None, "area", "harm", None, None),
        P(None, "area", "harm", None, None),
        P(None, "area", "harm", None, None),
        P("area", None),
        P("area"),
        P("area", None),
        P("area", None),
        P("area", None),
        P("area", None, None),
        P("area", None),
        P("area", None),
        P("area", None),
    )
    out_specs = P(None, "area", "harm", None, None)
    return jax.shard_map(
        per_device, mesh=mesh, in_specs=in_specs, out_specs=out_specs, check_vma=False
    )
```

```python
import functools
import math

import jax
import jax.numpy as jnp
import numpy as np
from jax import lax
from jax.experimental import pallas as pl
from jax.experimental.pallas import tpu as pltpu
from jax.sharding import PartitionSpec as P

NB = 768
NBD = 128
H = 28
TS = 512
HALF = TS // 2
CAP = 2048
SCEN = 32
PEER_CAP = 16
RANKS = 4
HL = H // RANKS
CH = 2 * HL
ROWS = RANKS * CH
SL = SCEN // RANKS
LANES = 128
CHUNKS = NB // LANES
BLOCK = 256
SIDE = 256

MESH = pl.DeviceIdType.MESH
F32 = jnp.float32
BF16 = jnp.bfloat16


def phase_tables():
    samples = np.arange(HALF)[:, None]
    columns = []
    for rank in range(RANKS):
        orders = 2 * (rank * HL + np.arange(HL))[None, :] + 1
        angles = (samples * orders % TS) * (2.0 * math.pi / TS)
        columns += [np.cos(angles), -np.sin(angles)]
    table = np.concatenate(columns, axis=1)

    def split(values):
        high = values.astype(np.float32).astype(BF16)
        low = (values - high.astype(np.float64)).astype(np.float32).astype(BF16)
        return high, low

    high, low = split(2.0 * table)
    synthesis = np.concatenate([high, high, low], axis=1)
    high, low = split((4.0 / TS) * table.T)
    analysis = np.concatenate([high, low], axis=0)
    return jnp.asarray(synthesis), jnp.asarray(analysis)


def split_two(values):
    high = values.astype(BF16).astype(F32)
    return high, values - high


def dot_rows(left, right):
    return lax.dot_general(
        left, right, (((1,), (1,)), ((), ())), preferred_element_type=F32
    )


def kernel(
    areas,
    ties,
    count_ref,
    volt_h,
    inject_h,
    zinv_h,
    bus_h,
    cond_h,
    sat_h,
    tarea_h,
    tbus_h,
    tfar_h,
    tres_h,
    treac_h,
    synth_h,
    anal_h,
    out_ref,
    volt_v,
    inject_v,
    zinv_v,
    bus_v,
    cond_v,
    sat_v,
    tarea_v,
    tbus_v,
    tfar_v,
    tres_v,
    treac_v,
    synth_v,
    anal_v,
    fwd_v,
    res_v,
    ret_v,
    req_s,
    req_r,
    tie_s,
    tie_r,
    adm_v,
    place_v,
    tie_v,
    load_sem,
    zinv_sem,
    self_sem,
    fs_sem,
    fr_sem,
    bs_sem,
    br_sem,
    qs_sem,
    qr_sem,
    ts_sem,
    tr_sem,
):
    slots = areas * PEER_CAP
    area = lax.axis_index("area")
    rank = lax.axis_index("harm")

    barrier = pltpu.get_barrier_semaphore()
    for step in range(1, RANKS):
        pl.semaphore_signal(
            barrier, inc=1, device_id=(area, (rank + step) % RANKS), device_id_type=MESH
        )

    def greet(step, carry):
        pl.semaphore_signal(
            barrier, inc=1, device_id=((area + step) % areas, rank), device_id_type=MESH
        )
        return carry

    lax.fori_loop(1, areas, greet, 0)

    pairs = [
        (tarea_h, tarea_v),
        (tbus_h, tbus_v),
        (tfar_h, tfar_v),
        (tres_h, tres_v),
        (treac_h, treac_v),
        (volt_h, volt_v),
        (bus_h, bus_v),
        (cond_h, cond_v),
        (sat_h, sat_v),
        (synth_h, synth_v),
        (anal_h, anal_v),
        (inject_h, inject_v),
    ]
    loads = [
        pltpu.make_async_copy(source, target, load_sem.at[i])
        for i, (source, target) in enumerate(pairs)
    ]
    for load in loads:
        load.start()

    def rank_rows(which):
        return pl.ds(which * CH, CH)

    def scenarios(which):
        return pl.ds(pl.multiple_of(which * SL, SL), SL)

    def lanes(chunk):
        return pl.ds(pl.multiple_of(chunk * LANES, LANES), LANES)

    def own_forward(chunk):
        return pltpu.make_async_copy(
            volt_h.at[:, scenarios(rank), lanes(chunk)],
            fwd_v.at[chunk, rank_rows(rank)],
            self_sem.at[chunk],
        )

    for chunk in range(CHUNKS):
        own_forward(chunk).start()

    order = (1, 2, 0)

    def zinv_copy(block):
        return pltpu.make_async_copy(
            zinv_h.at[:, :, pl.ds(block * BLOCK, BLOCK)],
            zinv_v.at[:, :, pl.ds(block * BLOCK, BLOCK)],
            zinv_sem.at[block],
        )

    for block in order:
        zinv_copy(block).start()

    for load in loads[:5]:
        load.wait()
    tie_rows = lax.broadcasted_iota(jnp.int32, (ties, ties), 0)
    tie_cols = lax.broadcasted_iota(jnp.int32, (ties, ties), 1)
    named = jnp.broadcast_to(tarea_v[...], (ties, ties))
    named_column = jnp.sum(
        jnp.where(tie_rows == tie_cols, named, 0), axis=1, keepdims=True
    )
    earlier = jnp.sum(
        jnp.where((named == named_column) & (tie_rows < tie_cols), 1, 0),
        axis=0,
        keepdims=True,
    )
    slot_row = tarea_v[...] * PEER_CAP + earlier
    slot_ids = lax.broadcasted_iota(jnp.int32, (slots, ties), 0)
    placed = jnp.where(slot_row == slot_ids, 1.0, 0.0).astype(BF16)
    bus_ids = lax.broadcasted_iota(jnp.int32, (NBD, ties), 0)
    far_pick = jnp.where(tfar_v[...] == bus_ids, 1.0, 0.0).astype(BF16)
    req_s[...] = dot_rows(placed, far_pick).reshape(areas, PEER_CAP, NBD)

    loads[5].wait()
    pl.semaphore_wait(barrier, RANKS - 1 + areas - 1)

    def forward(chunk, step):
        target = (rank + step) % RANKS
        return pltpu.make_async_remote_copy(
            src_ref=volt_v.at[:, scenarios(target), lanes(chunk)],
            dst_ref=fwd_v.at[chunk, rank_rows(rank)],
            send_sem=fs_sem.at[chunk, step - 1],
            recv_sem=fr_sem.at[chunk, step - 1],
            device_id=(area, target),
            device_id_type=MESH,
        )

    def backward(chunk, step):
        target = (rank + step) % RANKS
        return pltpu.make_async_remote_copy(
            src_ref=res_v.at[chunk, rank_rows(target)],
            dst_ref=ret_v.at[:, scenarios(rank), lanes(chunk)],
            send_sem=bs_sem.at[chunk, step - 1],
            recv_sem=br_sem.at[chunk, step - 1],
            device_id=(area, target),
            device_id_type=MESH,
        )

    def own_backward(chunk):
        return pltpu.make_async_copy(
            res_v.at[chunk, rank_rows(rank)],
            ret_v.at[:, scenarios(rank), lanes(chunk)],
            self_sem.at[CHUNKS + chunk],
        )

    def request(step):
        target = (area + step) % areas
        return pltpu.make_async_remote_copy(
            src_ref=req_s.at[target],
            dst_ref=req_r.at[area],
            send_sem=qs_sem.at[step],
            recv_sem=qr_sem.at[step],
            device_id=(target, rank),
            device_id_type=MESH,
        )

    def answer(step):
        target = (area + step) % areas
        return pltpu.make_async_remote_copy(
            src_ref=tie_s.at[target],
            dst_ref=tie_r.at[area],
            send_sem=ts_sem.at[step],
            recv_sem=tr_sem.at[step],
            device_id=(target, rank),
            device_id_type=MESH,
        )

    def each_area(action):
        def run(step, carry):
            action(step)
            return carry

        lax.fori_loop(1, areas, run, 0)

    def nth(i):
        return (i + 2) % CHUNKS

    def send_forward(i, carry):
        for step in (2, 1, 3):
            forward(nth(i), step).start()
        return carry

    lax.fori_loop(0, CHUNKS, send_forward, 0)
    each_area(lambda step: request(step).start())
    own_request = pltpu.make_async_copy(
        req_s.at[area], req_r.at[area], self_sem.at[2 * CHUNKS]
    )
    own_request.start()

    tie_bus_pick = jnp.where(tbus_v[...] == bus_ids, 1.0, 0.0).astype(BF16)
    place_v[...] = dot_rows(tie_bus_pick, placed).astype(BF16)
    resist_high, resist_low = split_two(tres_v[...])
    react_high, react_low = split_two(treac_v[...])
    line = lax.broadcasted_iota(jnp.int32, (8, ties), 0)
    columns = jnp.where(line == 0, resist_high, jnp.where(line == 1, resist_low, 0.0))
    columns = jnp.where(line == 2, react_high, jnp.where(line == 3, react_low, columns))
    columns = jnp.where(line == 4, 1.0, columns).astype(BF16)
    at_slot = dot_rows(placed, columns)
    resist = at_slot[:, 0:1] + at_slot[:, 1:2] + (1.0 - at_slot[:, 4:5])
    lane_ids = lax.broadcasted_iota(jnp.int32, (1, SIDE), 1)
    orders = (2 * (rank * HL + lane_ids // SCEN) + 1).astype(F32)
    reactance = (at_slot[:, 2:3] + at_slot[:, 3:4]) * orders
    denominator = resist * resist + reactance * reactance
    adm_v[0] = resist / denominator
    adm_v[1] = -reactance / denominator

    for load in loads[6:9]:
        load.wait()
    totals = jnp.zeros((8, NB), F32)
    line = lax.broadcasted_iota(jnp.int32, (8, BLOCK), 0)
    for part in range(CAP // BLOCK):
        here = slice(part * BLOCK, (part + 1) * BLOCK)
        slot = part * BLOCK + lax.broadcasted_iota(jnp.int32, (1, BLOCK), 1)
        live = jnp.where(slot < count_ref[0], 1.0, 0.0)
        rows = []
        for values in (cond_v[:, here], sat_v[:, here]):
            high, rest = split_two(live * values)
            middle, low = split_two(rest)
            rows += [high, middle, low]
        coefficients = jnp.zeros((8, BLOCK), F32)
        for i, row in enumerate(rows):
            coefficients = jnp.where(line == i, row, coefficients)
        bus_rows = lax.broadcasted_iota(jnp.int32, (NB, BLOCK), 0)
        pick = jnp.where(bus_v[:, here] == bus_rows, 1.0, 0.0).astype(BF16)
        totals = totals + dot_rows(coefficients.astype(BF16), pick)
    conductance = totals[0:1] + totals[1:2] + totals[2:3]
    saturation = totals[3:4] + totals[4:5] + totals[5:6]

    for load in loads[9:]:
        load.wait()

    def law(i, carry):
        chunk = nth(i)
        own_forward(chunk).wait()
        for step in range(1, RANKS):
            forward(chunk, step).wait_recv()
        for s in range(0, SL, 2):
            pair = jnp.concatenate(
                [
                    fwd_v[chunk, :, s, :],
                    fwd_v[chunk, :, s + 1, :],
                ],
                axis=1,
            )
            high, low = split_two(pair)
            stacked = jnp.concatenate([high, low, high], axis=0).astype(BF16)
            wave = jnp.dot(synth_v[...], stacked, preferred_element_type=F32)
            shape = jnp.tanh(wave).astype(BF16)
            both = jnp.dot(anal_v[...], shape, preferred_element_type=F32)
            harmonics = both[:ROWS] + both[ROWS:]
            res_v[chunk, :, s, :] = harmonics[:, :LANES]
            res_v[chunk, :, s + 1, :] = harmonics[:, LANES:]
        for step in (2, 1, 3):
            backward(chunk, step).start()
        own_backward(chunk).start()
        return carry

    lax.fori_loop(0, 2, law, 0)

    each_area(lambda step: request(step).wait_recv())
    own_request.wait()
    wanted = req_r[...].reshape(slots, NBD).astype(BF16)
    wanted = jnp.concatenate([wanted, wanted], axis=1)
    for part in range(2):
        edge = volt_v[part * HL : (part + 1) * HL, :, :NBD].reshape(HL * SCEN, NBD)
        high, low = split_two(edge)
        edge = jnp.concatenate([high, low], axis=1).astype(BF16)
        edge = jnp.concatenate(
            [edge, jnp.zeros((SIDE - HL * SCEN, 2 * NBD), BF16)], axis=0
        )
        tie_s[:, :, part * SIDE : (part + 1) * SIDE] = dot_rows(wanted, edge).reshape(
            areas, PEER_CAP, SIDE
        )
    each_area(lambda step: answer(step).start())
    own_answer = pltpu.make_async_copy(
        tie_s.at[area], tie_r.at[area], self_sem.at[2 * CHUNKS + 1]
    )
    own_answer.start()

    lax.fori_loop(2, CHUNKS, law, 0)

    for place, block in enumerate(order):
        zinv_copy(block).wait()
        for chunk in (2 * block, 2 * block + 1):
            own_backward(chunk).wait()
            for step in range(1, RANKS):
                backward(chunk, step).wait_recv()
        if block == 0:
            each_area(lambda step: answer(step).wait_recv())
            own_answer.wait()
            far = tie_r[...].reshape(slots, 2 * SIDE)
            far_real, far_imag = far[:, :SIDE], far[:, SIDE:]
            adm_real, adm_imag = adm_v[0], adm_v[1]
            for part, value in enumerate(
                (
                    adm_real * far_real - adm_imag * far_imag,
                    adm_real * far_imag + adm_imag * far_real,
                )
            ):
                high, low = split_two(value)
                summed = jnp.dot(
                    place_v[...], high.astype(BF16), preferred_element_type=F32
                ) + jnp.dot(place_v[...], low.astype(BF16), preferred_element_type=F32)
                tie_v[part] = summed.T
        here = slice(block * BLOCK, (block + 1) * BLOCK)
        for h in range(HL):
            sides = []
            for part in range(2):
                row = part * HL + h
                value = (
                    inject_v[row, :, here]
                    + conductance[:, here] * volt_v[row, :, here]
                    + saturation[:, here] * ret_v[row, :, here]
                )
                if block == 0:
                    tie = tie_v[part, h * SCEN : (h + 1) * SCEN, :]
                    value = jnp.concatenate(
                        [value[:, :NBD] + tie, value[:, NBD:]], axis=1
                    )
                sides.append(value)
            real, imag = sides
            straight = jnp.concatenate([real, imag], axis=0).astype(BF16)
            turned = jnp.concatenate([-imag, real], axis=0).astype(BF16)
            total = dot_rows(straight, zinv_v[h, :, here]) + dot_rows(
                turned, zinv_v[HL + h, :, here]
            )
            if place == 0:
                out_ref[h] = total[:SCEN]
                out_ref[HL + h] = total[SCEN:]
            else:
                out_ref[h] += total[:SCEN]
                out_ref[HL + h] += total[SCEN:]

    def drain(i, carry):
        for step in range(1, RANKS):
            forward(i, step).wait_send()
            backward(i, step).wait_send()
        return carry

    lax.fori_loop(0, CHUNKS, drain, 0)
    each_area(lambda step: request(step).wait_send())
    each_area(lambda step: answer(step).wait_send())


def per_device(
    volt,
    inject,
    zinv,
    dev_bus,
    dev_count,
    dev_cond,
    dev_sat,
    tie_bus,
    tie_area,
    tie_far,
    tie_res,
    tie_reac,
):
    areas = lax.axis_size("area")
    ties = tie_bus.shape[1]
    slots = areas * PEER_CAP
    synthesis, analysis = phase_tables()
    anywhere = pl.BlockSpec(memory_space=pl.ANY)
    dma = pltpu.SemaphoreType.DMA
    out = pl.pallas_call(
        functools.partial(kernel, areas, ties),
        out_shape=jax.ShapeDtypeStruct((CH, SCEN, NB), F32),
        in_specs=[pl.BlockSpec(memory_space=pltpu.SMEM)] + [anywhere] * 13,
        out_specs=pl.BlockSpec(memory_space=pltpu.VMEM),
        scratch_shapes=[
            pltpu.VMEM((CH, SCEN, NB), F32),
            pltpu.VMEM((CH, SCEN, NB), F32),
            pltpu.VMEM((CH, NB, NB), BF16),
            pltpu.VMEM((1, CAP), jnp.int32),
            pltpu.VMEM((1, CAP), F32),
            pltpu.VMEM((1, CAP), F32),
            pltpu.VMEM((1, ties), jnp.int32),
            pltpu.VMEM((1, ties), jnp.int32),
            pltpu.VMEM((1, ties), jnp.int32),
            pltpu.VMEM((1, ties), F32),
            pltpu.VMEM((1, ties), F32),
            pltpu.VMEM(synthesis.shape, BF16),
            pltpu.VMEM(analysis.shape, BF16),
            pltpu.VMEM((CHUNKS, ROWS, SL, LANES), F32),
            pltpu.VMEM((CHUNKS, ROWS, SL, LANES), F32),
            pltpu.VMEM((CH, SCEN, NB), F32),
            pltpu.VMEM((areas, PEER_CAP, NBD), F32),
            pltpu.VMEM((areas, PEER_CAP, NBD), F32),
            pltpu.VMEM((areas, PEER_CAP, 2 * SIDE), F32),
            pltpu.VMEM((areas, PEER_CAP, 2 * SIDE), F32),
            pltpu.VMEM((2, slots, SIDE), F32),
            pltpu.VMEM((NBD, slots), BF16),
            pltpu.VMEM((2, SIDE, NBD), F32),
            dma((12,)),
            dma((NB // BLOCK,)),
            dma((2 * CHUNKS + 2,)),
            dma((CHUNKS, RANKS - 1)),
            dma((CHUNKS, RANKS - 1)),
            dma((CHUNKS, RANKS - 1)),
            dma((CHUNKS, RANKS - 1)),
            dma((areas,)),
            dma((areas,)),
            dma((areas,)),
            dma((areas,)),
        ],
        compiler_params=pltpu.CompilerParams(
            collective_id=0, has_side_effects=True, vmem_limit_bytes=60 << 20
        ),
        name="sweep",
    )(
        dev_count,
        volt.reshape(CH, SCEN, NB),
        inject.reshape(CH, SCEN, NB),
        zinv.reshape(CH, NB, NB),
        dev_bus,
        dev_cond,
        dev_sat,
        tie_area.reshape(1, ties),
        tie_bus,
        tie_far,
        tie_res,
        tie_reac,
        synthesis,
        analysis,
    )
    return out.reshape(2, 1, HL, SCEN, NB)


def solution(mesh):
    in_specs = (
        P(None, "area", "harm", None, None),
        P(None, "area", "harm", None, None),
        P(None, "area", "harm", None, None),
        P("area", None),
        P("area"),
        P("area", None),
        P("area", None),
        P("area", None),
        P("area", None, None),
        P("area", None),
        P("area", None),
        P("area", None),
    )
    out_specs = P(None, "area", "harm", None, None)
    return jax.shard_map(
        per_device, mesh=mesh, in_specs=in_specs, out_specs=out_specs, check_vma=False
    )
```

```python
import functools
import math

import jax
import jax.numpy as jnp
import numpy as np
from jax import lax
from jax.experimental import pallas as pl
from jax.experimental.pallas import tpu as pltpu
from jax.sharding import PartitionSpec as P

NB = 768
NBD = 128
H = 28
TS = 512
HALF = TS // 2
CAP = 2048
SCEN = 32
PEER_CAP = 16
RANKS = 4
HL = H // RANKS
CH = 2 * HL
ROWS = RANKS * CH
SL = SCEN // RANKS
LANES = 128
CHUNKS = NB // LANES
BLOCK = 256
SIDE = 256

MESH = pl.DeviceIdType.MESH
F32 = jnp.float32
BF16 = jnp.bfloat16


def phase_tables():
    samples = np.arange(HALF)[:, None]
    columns = []
    for rank in range(RANKS):
        orders = 2 * (rank * HL + np.arange(HL))[None, :] + 1
        angles = (samples * orders % TS) * (2.0 * math.pi / TS)
        columns += [np.cos(angles), -np.sin(angles)]
    table = np.concatenate(columns, axis=1)

    def split(values):
        high = values.astype(np.float32).astype(BF16)
        low = (values - high.astype(np.float64)).astype(np.float32).astype(BF16)
        return high, low

    high, low = split(2.0 * table)
    synthesis = np.concatenate([high, high, low], axis=1)
    high, low = split((4.0 / TS) * table.T)
    analysis = np.concatenate([high, low], axis=0)
    return jnp.asarray(synthesis), jnp.asarray(analysis)


def split_two(values):
    high = values.astype(BF16).astype(F32)
    return high, values - high


def dot_rows(left, right):
    return lax.dot_general(
        left, right, (((1,), (1,)), ((), ())), preferred_element_type=F32
    )


def kernel(
    areas,
    ties,
    groups,
    count_ref,
    volt_h,
    inject_h,
    zinv_h,
    bus_h,
    cond_h,
    sat_h,
    tarea_h,
    tbus_h,
    tfar_h,
    tres_h,
    treac_h,
    synth_h,
    anal_h,
    out_ref,
    volt_v,
    inject_v,
    zinv_v,
    bus_v,
    cond_v,
    sat_v,
    tarea_v,
    tbus_v,
    tfar_v,
    tres_v,
    treac_v,
    synth_v,
    anal_v,
    fwd_v,
    res_v,
    ret_v,
    req_s,
    req_r,
    tie_s,
    tie_r,
    adm_v,
    place_v,
    tie_v,
    load_sem,
    zinv_sem,
    self_sem,
    fs_sem,
    fr_sem,
    bs_sem,
    br_sem,
    qs_sem,
    qr_sem,
    ts_sem,
    tr_sem,
    plane_sem,
):
    slots = areas * PEER_CAP
    area = lax.axis_index("area")
    rank = lax.axis_index("harm")

    barrier = pltpu.get_barrier_semaphore()
    for step in range(1, RANKS):
        pl.semaphore_signal(
            barrier, inc=1, device_id=(area, (rank + step) % RANKS), device_id_type=MESH
        )

    line = areas // groups
    base = area // line * line
    for step in range(1, line):
        peer = base + (area - base + step) % line
        pl.semaphore_signal(barrier, inc=1, device_id=(peer, rank), device_id_type=MESH)
    for step in range(1, groups):
        peer = (area + step * line) % areas
        pl.semaphore_signal(barrier, inc=1, device_id=(peer, rank), device_id_type=MESH)

    pairs = [
        (tarea_h, tarea_v),
        (tbus_h, tbus_v),
        (tfar_h, tfar_v),
        (tres_h, tres_v),
        (treac_h, treac_v),
        (volt_h, volt_v),
        (bus_h, bus_v),
        (cond_h, cond_v),
        (sat_h, sat_v),
        (synth_h, synth_v),
        (anal_h, anal_v),
        (inject_h, inject_v),
    ]
    loads = [
        pltpu.make_async_copy(source, target, load_sem.at[i])
        for i, (source, target) in enumerate(pairs)
    ]
    for load in loads:
        load.start()

    def rank_rows(which):
        return pl.ds(which * CH, CH)

    def scenarios(which):
        return pl.ds(pl.multiple_of(which * SL, SL), SL)

    def lanes(chunk):
        return pl.ds(pl.multiple_of(chunk * LANES, LANES), LANES)

    def own_forward(chunk):
        return pltpu.make_async_copy(
            volt_h.at[:, scenarios(rank), lanes(chunk)],
            fwd_v.at[chunk, rank_rows(rank)],
            self_sem.at[chunk],
        )

    for chunk in range(CHUNKS):
        own_forward(chunk).start()

    order = (1, 2, 0)

    def zinv_copy(block):
        return pltpu.make_async_copy(
            zinv_h.at[:, :, pl.ds(block * BLOCK, BLOCK)],
            zinv_v.at[:, :, pl.ds(block * BLOCK, BLOCK)],
            zinv_sem.at[block],
        )

    for block in order:
        zinv_copy(block).start()

    pl.semaphore_wait(barrier, RANKS - 1 + line - 1 + groups - 1)

    def forward(chunk, step):
        target = (rank + step) % RANKS
        return pltpu.make_async_remote_copy(
            src_ref=volt_h.at[:, scenarios(target), lanes(chunk)],
            dst_ref=fwd_v.at[chunk, rank_rows(rank)],
            send_sem=fs_sem.at[chunk, step - 1],
            recv_sem=fr_sem.at[chunk, step - 1],
            device_id=(area, target),
            device_id_type=MESH,
        )

    def backward(chunk, step):
        target = (rank + step) % RANKS
        return pltpu.make_async_remote_copy(
            src_ref=res_v.at[chunk, rank_rows(target)],
            dst_ref=ret_v.at[:, scenarios(rank), lanes(chunk)],
            send_sem=bs_sem.at[chunk, step - 1],
            recv_sem=br_sem.at[chunk, step - 1],
            device_id=(area, target),
            device_id_type=MESH,
        )

    def own_backward(chunk):
        return pltpu.make_async_copy(
            res_v.at[chunk, rank_rows(rank)],
            ret_v.at[:, scenarios(rank), lanes(chunk)],
            self_sem.at[CHUNKS + chunk],
        )

    def request(step):
        target = (area + step) % areas
        return pltpu.make_async_remote_copy(
            src_ref=req_s.at[target],
            dst_ref=req_r.at[area],
            send_sem=qs_sem.at[step],
            recv_sem=qr_sem.at[step],
            device_id=(target, rank),
            device_id_type=MESH,
        )

    def answer(step):
        target = (area + step) % areas
        return pltpu.make_async_remote_copy(
            src_ref=tie_s.at[target],
            dst_ref=tie_r.at[area],
            send_sem=ts_sem.at[step],
            recv_sem=tr_sem.at[step],
            device_id=(target, rank),
            device_id_type=MESH,
        )

    def each_area(action):
        def run(step, carry):
            action(step)
            return carry

        lax.fori_loop(1, areas, run, 0)

    def nth(i):
        return (i + 2) % CHUNKS

    def send_forward(i, carry):
        for step in (2, 1, 3):
            forward(nth(i), step).start()
        return carry

    lax.fori_loop(0, CHUNKS, send_forward, 0)
    for step in range(1, groups):
        peer = (area + step * line) % areas
        pl.semaphore_signal(
            plane_sem, inc=1, device_id=(peer, rank), device_id_type=MESH
        )

    for load in loads[:5]:
        load.wait()
    tie_rows = lax.broadcasted_iota(jnp.int32, (ties, ties), 0)
    tie_cols = lax.broadcasted_iota(jnp.int32, (ties, ties), 1)
    named = jnp.broadcast_to(tarea_v[...], (ties, ties))
    named_column = jnp.sum(
        jnp.where(tie_rows == tie_cols, named, 0), axis=1, keepdims=True
    )
    earlier = jnp.sum(
        jnp.where((named == named_column) & (tie_rows < tie_cols), 1, 0),
        axis=0,
        keepdims=True,
    )
    slot_row = tarea_v[...] * PEER_CAP + earlier
    slot_ids = lax.broadcasted_iota(jnp.int32, (slots, ties), 0)
    placed = jnp.where(slot_row == slot_ids, 1.0, 0.0).astype(BF16)
    bus_ids = lax.broadcasted_iota(jnp.int32, (NBD, ties), 0)
    far_pick = jnp.where(tfar_v[...] == bus_ids, 1.0, 0.0).astype(BF16)
    req_s[...] = dot_rows(placed, far_pick).reshape(areas, PEER_CAP, NBD)

    pl.semaphore_wait(plane_sem, groups - 1)
    each_area(lambda step: request(step).start())
    own_request = pltpu.make_async_copy(
        req_s.at[area], req_r.at[area], self_sem.at[2 * CHUNKS]
    )
    own_request.start()

    tie_bus_pick = jnp.where(tbus_v[...] == bus_ids, 1.0, 0.0).astype(BF16)
    place_v[...] = dot_rows(tie_bus_pick, placed).astype(BF16)
    resist_high, resist_low = split_two(tres_v[...])
    react_high, react_low = split_two(treac_v[...])
    row_ids = lax.broadcasted_iota(jnp.int32, (8, ties), 0)
    columns = jnp.where(row_ids == 0, resist_high, jnp.where(row_ids == 1, resist_low, 0.0))
    columns = jnp.where(row_ids == 2, react_high, jnp.where(row_ids == 3, react_low, columns))
    columns = jnp.where(row_ids == 4, 1.0, columns).astype(BF16)
    at_slot = dot_rows(placed, columns)
    resist = at_slot[:, 0:1] + at_slot[:, 1:2] + (1.0 - at_slot[:, 4:5])
    lane_ids = lax.broadcasted_iota(jnp.int32, (1, SIDE), 1)
    orders = (2 * (rank * HL + lane_ids // SCEN) + 1).astype(F32)
    reactance = (at_slot[:, 2:3] + at_slot[:, 3:4]) * orders
    denominator = resist * resist + reactance * reactance
    adm_v[0] = resist / denominator
    adm_v[1] = -reactance / denominator

    for load in loads[6:9]:
        load.wait()
    totals = jnp.zeros((8, NB), F32)
    row_ids = lax.broadcasted_iota(jnp.int32, (8, BLOCK), 0)
    for part in range(CAP // BLOCK):
        here = slice(part * BLOCK, (part + 1) * BLOCK)
        slot = part * BLOCK + lax.broadcasted_iota(jnp.int32, (1, BLOCK), 1)
        live = jnp.where(slot < count_ref[0], 1.0, 0.0)
        rows = []
        for values in (cond_v[:, here], sat_v[:, here]):
            high, rest = split_two(live * values)
            middle, low = split_two(rest)
            rows += [high, middle, low]
        coefficients = jnp.zeros((8, BLOCK), F32)
        for i, row in enumerate(rows):
            coefficients = jnp.where(row_ids == i, row, coefficients)
        bus_rows = lax.broadcasted_iota(jnp.int32, (NB, BLOCK), 0)
        pick = jnp.where(bus_v[:, here] == bus_rows, 1.0, 0.0).astype(BF16)
        totals = totals + dot_rows(coefficients.astype(BF16), pick)
    conductance = totals[0:1] + totals[1:2] + totals[2:3]
    saturation = totals[3:4] + totals[4:5] + totals[5:6]

    for load in loads[9:]:
        load.wait()
    loads[5].wait()

    def law(i, carry):
        chunk = nth(i)
        own_forward(chunk).wait()
        for step in range(1, RANKS):
            forward(chunk, step).wait_recv()
        for s in range(0, SL, 2):
            pair = jnp.concatenate(
                [
                    fwd_v[chunk, :, s, :],
                    fwd_v[chunk, :, s + 1, :],
                ],
                axis=1,
            )
            high, low = split_two(pair)
            stacked = jnp.concatenate([high, low, high], axis=0).astype(BF16)
            wave = jnp.dot(synth_v[...], stacked, preferred_element_type=F32)
            shape = jnp.tanh(wave).astype(BF16)
            both = jnp.dot(anal_v[...], shape, preferred_element_type=F32)
            harmonics = both[:ROWS] + both[ROWS:]
            res_v[chunk, :, s, :] = harmonics[:, :LANES]
            res_v[chunk, :, s + 1, :] = harmonics[:, LANES:]
        for step in (2, 1, 3):
            backward(chunk, step).start()
        own_backward(chunk).start()
        return carry

    lax.fori_loop(0, 2, law, 0)

    each_area(lambda step: request(step).wait_recv())
    own_request.wait()
    wanted = req_r[...].reshape(slots, NBD).astype(BF16)
    wanted = jnp.concatenate([wanted, wanted], axis=1)
    for part in range(2):
        edge = volt_v[part * HL : (part + 1) * HL, :, :NBD].reshape(HL * SCEN, NBD)
        high, low = split_two(edge)
        edge = jnp.concatenate([high, low], axis=1).astype(BF16)
        edge = jnp.concatenate(
            [edge, jnp.zeros((SIDE - HL * SCEN, 2 * NBD), BF16)], axis=0
        )
        tie_s[:, :, part * SIDE : (part + 1) * SIDE] = dot_rows(wanted, edge).reshape(
            areas, PEER_CAP, SIDE
        )
    each_area(lambda step: answer(step).start())
    own_answer = pltpu.make_async_copy(
        tie_s.at[area], tie_r.at[area], self_sem.at[2 * CHUNKS + 1]
    )
    own_answer.start()

    lax.fori_loop(2, CHUNKS, law, 0)

    def result_in(chunk):
        own_backward(chunk).wait()
        for step in range(1, RANKS):
            backward(chunk, step).wait_recv()

    def gather_ties():
        each_area(lambda step: answer(step).wait_recv())
        own_answer.wait()
        far = tie_r[...].reshape(slots, 2 * SIDE)
        far_real, far_imag = far[:, :SIDE], far[:, SIDE:]
        adm_real, adm_imag = adm_v[0], adm_v[1]
        for part, value in enumerate(
            (
                adm_real * far_real - adm_imag * far_imag,
                adm_real * far_imag + adm_imag * far_real,
            )
        ):
            high, low = split_two(value)
            summed = jnp.dot(
                place_v[...], high.astype(BF16), preferred_element_type=F32
            ) + jnp.dot(place_v[...], low.astype(BF16), preferred_element_type=F32)
            tie_v[part] = summed.T

    def accumulate(first, chunks, fresh):
        here = slice(first * LANES, (first + chunks) * LANES)
        for h in range(HL):
            sides = []
            for part in range(2):
                row = part * HL + h
                value = (
                    inject_v[row, :, here]
                    + conductance[:, here] * volt_v[row, :, here]
                    + saturation[:, here] * ret_v[row, :, here]
                )
                if first == 0:
                    value = value + tie_v[part, h * SCEN : (h + 1) * SCEN, :]
                sides.append(value)
            real, imag = sides
            straight = jnp.concatenate([real, imag], axis=0).astype(BF16)
            turned = jnp.concatenate([-imag, real], axis=0).astype(BF16)
            total = dot_rows(straight, zinv_v[h, :, here]) + dot_rows(
                turned, zinv_v[HL + h, :, here]
            )
            if fresh:
                out_ref[h] = total[:SCEN]
                out_ref[HL + h] = total[SCEN:]
            else:
                out_ref[h] += total[:SCEN]
                out_ref[HL + h] += total[SCEN:]

    for place, block in enumerate(order[:2]):
        zinv_copy(block).wait()
        result_in(2 * block)
        result_in(2 * block + 1)
        accumulate(2 * block, 2, place == 0)
    gather_ties()
    zinv_copy(0).wait()
    result_in(0)
    accumulate(0, 1, False)
    result_in(1)
    accumulate(1, 1, False)

    def drain(i, carry):
        for step in range(1, RANKS):
            forward(i, step).wait_send()
            backward(i, step).wait_send()
        return carry

    lax.fori_loop(0, CHUNKS, drain, 0)
    each_area(lambda step: request(step).wait_send())
    each_area(lambda step: answer(step).wait_send())


def per_device(
    volt,
    inject,
    zinv,
    dev_bus,
    dev_count,
    dev_cond,
    dev_sat,
    tie_bus,
    tie_area,
    tie_far,
    tie_res,
    tie_reac,
):
    areas = lax.axis_size("area")
    ties = tie_bus.shape[1]
    slots = areas * PEER_CAP
    synthesis, analysis = phase_tables()
    anywhere = pl.BlockSpec(memory_space=pl.ANY)
    dma = pltpu.SemaphoreType.DMA
    out = pl.pallas_call(
        functools.partial(kernel, areas, ties, 4 if areas > 8 else 2),
        out_shape=pltpu.VMEM((CH, SCEN, NB), F32),
        in_specs=[pl.BlockSpec(memory_space=pltpu.SMEM)] + [anywhere] * 13,
        out_specs=pl.BlockSpec(memory_space=pltpu.VMEM),
        scratch_shapes=[
            pltpu.VMEM((CH, SCEN, NB), F32),
            pltpu.VMEM((CH, SCEN, NB), F32),
            pltpu.VMEM((CH, NB, NB), BF16),
            pltpu.VMEM((1, CAP), jnp.int32),
            pltpu.VMEM((1, CAP), F32),
            pltpu.VMEM((1, CAP), F32),
            pltpu.VMEM((1, ties), jnp.int32),
            pltpu.VMEM((1, ties), jnp.int32),
            pltpu.VMEM((1, ties), jnp.int32),
            pltpu.VMEM((1, ties), F32),
            pltpu.VMEM((1, ties), F32),
            pltpu.VMEM(synthesis.shape, BF16),
            pltpu.VMEM(analysis.shape, BF16),
            pltpu.VMEM((CHUNKS, ROWS, SL, LANES), F32),
            pltpu.VMEM((CHUNKS, ROWS, SL, LANES), F32),
            pltpu.VMEM((CH, SCEN, NB), F32),
            pltpu.VMEM((areas, PEER_CAP, NBD), F32),
            pltpu.VMEM((areas, PEER_CAP, NBD), F32),
            pltpu.VMEM((areas, PEER_CAP, 2 * SIDE), F32),
            pltpu.VMEM((areas, PEER_CAP, 2 * SIDE), F32),
            pltpu.VMEM((2, slots, SIDE), F32),
            pltpu.VMEM((NBD, slots), BF16),
            pltpu.VMEM((2, SIDE, NBD), F32),
            dma((12,)),
            dma((NB // BLOCK,)),
            dma((2 * CHUNKS + 2,)),
            dma((CHUNKS, RANKS - 1)),
            dma((CHUNKS, RANKS - 1)),
            dma((CHUNKS, RANKS - 1)),
            dma((CHUNKS, RANKS - 1)),
            dma((areas,)),
            dma((areas,)),
            dma((areas,)),
            dma((areas,)),
            pltpu.SemaphoreType.REGULAR,
        ],
        compiler_params=pltpu.CompilerParams(
            collective_id=0, has_side_effects=True, vmem_limit_bytes=60 << 20
        ),
        name="sweep",
    )(
        dev_count,
        volt.reshape(CH, SCEN, NB),
        inject.reshape(CH, SCEN, NB),
        zinv.reshape(CH, NB, NB),
        dev_bus,
        dev_cond,
        dev_sat,
        tie_area.reshape(1, ties),
        tie_bus,
        tie_far,
        tie_res,
        tie_reac,
        synthesis,
        analysis,
    )
    return out.reshape(2, 1, HL, SCEN, NB)


def solution(mesh):
    in_specs = (
        P(None, "area", "harm", None, None),
        P(None, "area", "harm", None, None),
        P(None, "area", "harm", None, None),
        P("area", None),
        P("area"),
        P("area", None),
        P("area", None),
        P("area", None),
        P("area", None, None),
        P("area", None),
        P("area", None),
        P("area", None),
    )
    out_specs = P(None, "area", "harm", None, None)
    return jax.shard_map(
        per_device, mesh=mesh, in_specs=in_specs, out_specs=out_specs, check_vma=False
    )
```

```python
import functools
import math

import jax
import jax.numpy as jnp
import numpy as np
from jax import lax
from jax.experimental import pallas as pl
from jax.experimental.pallas import tpu as pltpu
from jax.sharding import PartitionSpec as P

NB = 768
NBD = 128
H = 28
TS = 512
HALF = TS // 2
CAP = 2048
SCEN = 32
PEER_CAP = 16
RANKS = 4
HL = H // RANKS
CH = 2 * HL
ROWS = RANKS * CH
SL = SCEN // RANKS
LANES = 128
CHUNKS = NB // LANES
BLOCK = 256
SIDE = 256

MESH = pl.DeviceIdType.MESH
F32 = jnp.float32
BF16 = jnp.bfloat16


def phase_tables():
    samples = np.arange(HALF)[:, None]
    columns = []
    for rank in range(RANKS):
        orders = 2 * (rank * HL + np.arange(HL))[None, :] + 1
        angles = (samples * orders % TS) * (2.0 * math.pi / TS)
        columns += [np.cos(angles), -np.sin(angles)]
    table = np.concatenate(columns, axis=1)

    def split(values):
        high = values.astype(np.float32).astype(BF16)
        low = (values - high.astype(np.float64)).astype(np.float32).astype(BF16)
        return high, low

    high, low = split(2.0 * table)
    synthesis = np.concatenate([high, high, low], axis=1)
    high, low = split((4.0 / TS) * table.T)
    analysis = np.concatenate([high, low], axis=0)
    return jnp.asarray(synthesis), jnp.asarray(analysis)


def split_two(values):
    high = values.astype(BF16).astype(F32)
    return high, values - high


def dot_rows(left, right):
    return lax.dot_general(
        left, right, (((1,), (1,)), ((), ())), preferred_element_type=F32
    )


def kernel(
    areas,
    ties,
    groups,
    count_ref,
    volt_h,
    inject_h,
    zinv_h,
    bus_h,
    cond_h,
    sat_h,
    tarea_h,
    tbus_h,
    tfar_h,
    tres_h,
    treac_h,
    synth_h,
    anal_h,
    out_ref,
    volt_v,
    inject_v,
    zinv_v,
    bus_v,
    cond_v,
    sat_v,
    tarea_v,
    tbus_v,
    tfar_v,
    tres_v,
    treac_v,
    synth_v,
    anal_v,
    fwd_v,
    res_v,
    ret_v,
    req_s,
    req_r,
    tie_s,
    tie_r,
    adm_v,
    place_v,
    tie_v,
    load_sem,
    zinv_sem,
    self_sem,
    fs_sem,
    fr_sem,
    bs_sem,
    br_sem,
    qs_sem,
    qr_sem,
    ts_sem,
    tr_sem,
    entry_sem,
    plane_sem,
):
    slots = areas * PEER_CAP
    area = lax.axis_index("area")
    rank = lax.axis_index("harm")

    barrier = pltpu.get_barrier_semaphore()
    for step in range(1, RANKS):
        pl.semaphore_signal(
            barrier, inc=1, device_id=(area, (rank + step) % RANKS), device_id_type=MESH
        )

    line = areas // groups
    base = area // line * line
    group = area // line
    place = area - base

    def greet(semaphore, sign):
        for step in range(1, line):
            near = place + sign * step

            @pl.when((near >= 0) & (near < line))
            def _():
                pl.semaphore_signal(
                    semaphore, inc=1, device_id=(base + near, rank), device_id_type=MESH
                )

        for step in range(1, groups):
            other = group + sign * step

            @pl.when((other >= 0) & (other < groups))
            def _():
                pl.semaphore_signal(
                    semaphore,
                    inc=1,
                    device_id=(other * line + place, rank),
                    device_id_type=MESH,
                )

    greet(barrier, 1)

    def rank_rows(which):
        return pl.ds(which * CH, CH)

    def scenarios(which):
        return pl.ds(pl.multiple_of(which * SL, SL), SL)

    def lanes(chunk):
        return pl.ds(pl.multiple_of(chunk * LANES, LANES), LANES)

    def own_forward(chunk):
        return pltpu.make_async_copy(
            volt_h.at[:, scenarios(rank), lanes(chunk)],
            fwd_v.at[chunk, rank_rows(rank)],
            self_sem.at[chunk],
        )

    pl.semaphore_wait(barrier, RANKS - 1 + place + group)

    def forward(chunk, step):
        target = (rank + step) % RANKS
        return pltpu.make_async_remote_copy(
            src_ref=volt_h.at[:, scenarios(target), lanes(chunk)],
            dst_ref=fwd_v.at[chunk, rank_rows(rank)],
            send_sem=fs_sem.at[chunk, step - 1],
            recv_sem=fr_sem.at[chunk, step - 1],
            device_id=(area, target),
            device_id_type=MESH,
        )

    def backward(chunk, step):
        target = (rank + step) % RANKS
        return pltpu.make_async_remote_copy(
            src_ref=res_v.at[chunk, rank_rows(target)],
            dst_ref=ret_v.at[:, scenarios(rank), lanes(chunk)],
            send_sem=bs_sem.at[chunk, step - 1],
            recv_sem=br_sem.at[chunk, step - 1],
            device_id=(area, target),
            device_id_type=MESH,
        )

    def own_backward(chunk):
        return pltpu.make_async_copy(
            res_v.at[chunk, rank_rows(rank)],
            ret_v.at[:, scenarios(rank), lanes(chunk)],
            self_sem.at[CHUNKS + chunk],
        )

    def request(step):
        target = (area + step) % areas
        return pltpu.make_async_remote_copy(
            src_ref=req_s.at[target],
            dst_ref=req_r.at[area],
            send_sem=qs_sem.at[step],
            recv_sem=qr_sem.at[step],
            device_id=(target, rank),
            device_id_type=MESH,
        )

    def answer(step):
        target = (area + step) % areas
        return pltpu.make_async_remote_copy(
            src_ref=tie_s.at[target],
            dst_ref=tie_r.at[area],
            send_sem=ts_sem.at[step],
            recv_sem=tr_sem.at[step],
            device_id=(target, rank),
            device_id_type=MESH,
        )

    def each_area(action):
        def run(step, carry):
            action(step)
            return carry

        lax.fori_loop(1, areas, run, 0)

    def nth(i):
        return (i + 2) % CHUNKS

    def send_forward(i, carry):
        for step in (2, 1, 3):
            forward(nth(i), step).start()
        return carry

    lax.fori_loop(0, CHUNKS, send_forward, 0)
    greet(entry_sem, -1)

    pairs = [
        (tarea_h, tarea_v),
        (tbus_h, tbus_v),
        (tfar_h, tfar_v),
        (tres_h, tres_v),
        (treac_h, treac_v),
        (volt_h, volt_v),
        (bus_h, bus_v),
        (cond_h, cond_v),
        (sat_h, sat_v),
        (synth_h, synth_v),
        (anal_h, anal_v),
        (inject_h, inject_v),
    ]
    loads = [
        pltpu.make_async_copy(source, target, load_sem.at[i])
        for i, (source, target) in enumerate(pairs)
    ]
    for load in loads:
        load.start()

    for chunk in range(CHUNKS):
        own_forward(chunk).start()

    order = (1, 2, 0)

    def zinv_copy(block):
        return pltpu.make_async_copy(
            zinv_h.at[:, :, pl.ds(block * BLOCK, BLOCK)],
            zinv_v.at[:, :, pl.ds(block * BLOCK, BLOCK)],
            zinv_sem.at[block],
        )

    for block in order:
        zinv_copy(block).start()

    for load in loads[:5]:
        load.wait()
    tie_rows = lax.broadcasted_iota(jnp.int32, (ties, ties), 0)
    tie_cols = lax.broadcasted_iota(jnp.int32, (ties, ties), 1)
    named = jnp.broadcast_to(tarea_v[...], (ties, ties))
    named_column = jnp.sum(
        jnp.where(tie_rows == tie_cols, named, 0), axis=1, keepdims=True
    )
    earlier = jnp.sum(
        jnp.where((named == named_column) & (tie_rows < tie_cols), 1, 0),
        axis=0,
        keepdims=True,
    )
    slot_row = tarea_v[...] * PEER_CAP + earlier
    slot_ids = lax.broadcasted_iota(jnp.int32, (slots, ties), 0)
    placed = jnp.where(slot_row == slot_ids, 1.0, 0.0).astype(BF16)
    bus_ids = lax.broadcasted_iota(jnp.int32, (NBD, ties), 0)
    area_ids = lax.broadcasted_iota(jnp.int32, (areas, ties), 0)
    of_area = jnp.where(tarea_v[...] == area_ids, 1.0, 0.0).astype(BF16)
    wish = (tfar_v[...] + 1).astype(F32)
    of_turn = jnp.where(earlier == bus_ids, wish, 0.0).astype(BF16)
    wishes = dot_rows(of_area, of_turn)
    req_s[...] = jnp.broadcast_to(wishes[:, None, :], (areas, 8, LANES))

    later = line - 1 - place + groups - 1 - group

    @pl.when(later > 0)
    def _():
        pl.semaphore_wait(entry_sem, later)

    for step in range(1, groups):
        peer = (area + step * line) % areas
        pl.semaphore_signal(
            plane_sem, inc=1, device_id=(peer, rank), device_id_type=MESH
        )
    pl.semaphore_wait(plane_sem, groups - 1)
    each_area(lambda step: request(step).start())
    own_request = pltpu.make_async_copy(
        req_s.at[area], req_r.at[area], self_sem.at[2 * CHUNKS]
    )
    own_request.start()

    tie_bus_pick = jnp.where(tbus_v[...] == bus_ids, 1.0, 0.0).astype(BF16)
    place_v[...] = dot_rows(tie_bus_pick, placed).astype(BF16)
    resist_high, resist_low = split_two(tres_v[...])
    react_high, react_low = split_two(treac_v[...])
    row_ids = lax.broadcasted_iota(jnp.int32, (8, ties), 0)
    columns = jnp.where(row_ids == 0, resist_high, jnp.where(row_ids == 1, resist_low, 0.0))
    columns = jnp.where(row_ids == 2, react_high, jnp.where(row_ids == 3, react_low, columns))
    columns = jnp.where(row_ids == 4, 1.0, columns).astype(BF16)
    at_slot = dot_rows(placed, columns)
    resist = at_slot[:, 0:1] + at_slot[:, 1:2] + (1.0 - at_slot[:, 4:5])
    lane_ids = lax.broadcasted_iota(jnp.int32, (1, SIDE), 1)
    orders = (2 * (rank * HL + lane_ids // SCEN) + 1).astype(F32)
    reactance = (at_slot[:, 2:3] + at_slot[:, 3:4]) * orders
    denominator = resist * resist + reactance * reactance
    adm_v[0] = resist / denominator
    adm_v[1] = -reactance / denominator

    for load in loads[6:9]:
        load.wait()
    totals = jnp.zeros((8, NB), F32)
    row_ids = lax.broadcasted_iota(jnp.int32, (8, BLOCK), 0)
    for part in range(CAP // BLOCK):
        here = slice(part * BLOCK, (part + 1) * BLOCK)
        slot = part * BLOCK + lax.broadcasted_iota(jnp.int32, (1, BLOCK), 1)
        live = jnp.where(slot < count_ref[0], 1.0, 0.0)
        rows = []
        for values in (cond_v[:, here], sat_v[:, here]):
            high, rest = split_two(live * values)
            middle, low = split_two(rest)
            rows += [high, middle, low]
        coefficients = jnp.zeros((8, BLOCK), F32)
        for i, row in enumerate(rows):
            coefficients = jnp.where(row_ids == i, row, coefficients)
        bus_rows = lax.broadcasted_iota(jnp.int32, (NB, BLOCK), 0)
        pick = jnp.where(bus_v[:, here] == bus_rows, 1.0, 0.0).astype(BF16)
        totals = totals + dot_rows(coefficients.astype(BF16), pick)
    conductance = totals[0:1] + totals[1:2] + totals[2:3]
    saturation = totals[3:4] + totals[4:5] + totals[5:6]

    for load in loads[9:]:
        load.wait()
    loads[5].wait()

    def law(i, carry):
        chunk = nth(i)
        own_forward(chunk).wait()
        for step in range(1, RANKS):
            forward(chunk, step).wait_recv()
        for s in range(0, SL, 2):
            pair = jnp.concatenate(
                [
                    fwd_v[chunk, :, s, :],
                    fwd_v[chunk, :, s + 1, :],
                ],
                axis=1,
            )
            high, low = split_two(pair)
            stacked = jnp.concatenate([high, low, high], axis=0).astype(BF16)
            wave = jnp.dot(synth_v[...], stacked, preferred_element_type=F32)
            shape = jnp.tanh(wave).astype(BF16)
            both = jnp.dot(anal_v[...], shape, preferred_element_type=F32)
            harmonics = both[:ROWS] + both[ROWS:]
            res_v[chunk, :, s, :] = harmonics[:, :LANES]
            res_v[chunk, :, s + 1, :] = harmonics[:, LANES:]
        for step in (2, 1, 3):
            backward(chunk, step).start()
        own_backward(chunk).start()
        return carry

    lax.fori_loop(0, 4, law, 0)

    each_area(lambda step: request(step).wait_recv())
    own_request.wait()
    asked = req_r[:, 0, :].astype(BF16)
    slot_rows = lax.broadcasted_iota(jnp.int32, (slots, areas), 0) // PEER_CAP
    slot_cols = lax.broadcasted_iota(jnp.int32, (slots, areas), 1)
    spread = jnp.where(slot_rows == slot_cols, 1.0, 0.0).astype(BF16)
    asked = jnp.dot(spread, asked, preferred_element_type=F32)
    turn_ids = lax.broadcasted_iota(jnp.int32, (slots, LANES), 0) % PEER_CAP
    far_ids = lax.broadcasted_iota(jnp.int32, (slots, LANES), 1)
    asked = jnp.sum(
        jnp.where(turn_ids == far_ids, asked, 0.0), axis=1, keepdims=True
    ).astype(jnp.int32)
    wanted = jnp.where(asked == far_ids + 1, 1.0, 0.0).astype(BF16)
    wanted = jnp.concatenate([wanted, wanted], axis=1)
    for part in range(2):
        edge = volt_v[part * HL : (part + 1) * HL, :, :NBD].reshape(HL * SCEN, NBD)
        high, low = split_two(edge)
        edge = jnp.concatenate([high, low], axis=1).astype(BF16)
        edge = jnp.concatenate(
            [edge, jnp.zeros((SIDE - HL * SCEN, 2 * NBD), BF16)], axis=0
        )
        tie_s[:, :, part * SIDE : (part + 1) * SIDE] = dot_rows(wanted, edge).reshape(
            areas, PEER_CAP, SIDE
        )
    each_area(lambda step: answer(step).start())
    own_answer = pltpu.make_async_copy(
        tie_s.at[area], tie_r.at[area], self_sem.at[2 * CHUNKS + 1]
    )
    own_answer.start()

    lax.fori_loop(4, CHUNKS, law, 0)

    def result_in(chunk):
        own_backward(chunk).wait()
        for step in range(1, RANKS):
            backward(chunk, step).wait_recv()

    def gather_ties():
        each_area(lambda step: answer(step).wait_recv())
        own_answer.wait()
        far = tie_r[...].reshape(slots, 2 * SIDE)
        far_real, far_imag = far[:, :SIDE], far[:, SIDE:]
        adm_real, adm_imag = adm_v[0], adm_v[1]
        for part, value in enumerate(
            (
                adm_real * far_real - adm_imag * far_imag,
                adm_real * far_imag + adm_imag * far_real,
            )
        ):
            high, low = split_two(value)
            summed = jnp.dot(
                place_v[...], high.astype(BF16), preferred_element_type=F32
            ) + jnp.dot(place_v[...], low.astype(BF16), preferred_element_type=F32)
            tie_v[part] = summed.T

    def accumulate(first, chunks, fresh):
        here = slice(first * LANES, (first + chunks) * LANES)
        for h in range(HL):
            sides = []
            for part in range(2):
                row = part * HL + h
                value = (
                    inject_v[row, :, here]
                    + conductance[:, here] * volt_v[row, :, here]
                    + saturation[:, here] * ret_v[row, :, here]
                )
                if first == 0:
                    value = value + tie_v[part, h * SCEN : (h + 1) * SCEN, :]
                sides.append(value)
            real, imag = sides
            straight = jnp.concatenate([real, imag], axis=0).astype(BF16)
            turned = jnp.concatenate([-imag, real], axis=0).astype(BF16)
            total = dot_rows(straight, zinv_v[h, :, here]) + dot_rows(
                turned, zinv_v[HL + h, :, here]
            )
            if fresh:
                out_ref[h] = total[:SCEN]
                out_ref[HL + h] = total[SCEN:]
            else:
                out_ref[h] += total[:SCEN]
                out_ref[HL + h] += total[SCEN:]

    for turn, block in enumerate(order[:2]):
        zinv_copy(block).wait()
        result_in(2 * block)
        result_in(2 * block + 1)
        accumulate(2 * block, 2, turn == 0)
    gather_ties()
    zinv_copy(0).wait()
    result_in(0)
    accumulate(0, 1, False)
    result_in(1)
    accumulate(1, 1, False)

    def drain(i, carry):
        for step in range(1, RANKS):
            forward(i, step).wait_send()
            backward(i, step).wait_send()
        return carry

    lax.fori_loop(0, CHUNKS, drain, 0)
    each_area(lambda step: request(step).wait_send())
    each_area(lambda step: answer(step).wait_send())


def per_device(
    volt,
    inject,
    zinv,
    dev_bus,
    dev_count,
    dev_cond,
    dev_sat,
    tie_bus,
    tie_area,
    tie_far,
    tie_res,
    tie_reac,
):
    areas = lax.axis_size("area")
    ties = tie_bus.shape[1]
    slots = areas * PEER_CAP
    synthesis, analysis = phase_tables()
    anywhere = pl.BlockSpec(memory_space=pl.ANY)
    dma = pltpu.SemaphoreType.DMA
    out = pl.pallas_call(
        functools.partial(kernel, areas, ties, 4 if areas > 8 else 2),
        out_shape=pltpu.VMEM((CH, SCEN, NB), F32),
        in_specs=[pl.BlockSpec(memory_space=pltpu.SMEM)] + [anywhere] * 13,
        out_specs=pl.BlockSpec(memory_space=pltpu.VMEM),
        scratch_shapes=[
            pltpu.VMEM((CH, SCEN, NB), F32),
            pltpu.VMEM((CH, SCEN, NB), F32),
            pltpu.VMEM((CH, NB, NB), BF16),
            pltpu.VMEM((1, CAP), jnp.int32),
            pltpu.VMEM((1, CAP), F32),
            pltpu.VMEM((1, CAP), F32),
            pltpu.VMEM((1, ties), jnp.int32),
            pltpu.VMEM((1, ties), jnp.int32),
            pltpu.VMEM((1, ties), jnp.int32),
            pltpu.VMEM((1, ties), F32),
            pltpu.VMEM((1, ties), F32),
            pltpu.VMEM(synthesis.shape, BF16),
            pltpu.VMEM(analysis.shape, BF16),
            pltpu.VMEM((CHUNKS, ROWS, SL, LANES), F32),
            pltpu.VMEM((CHUNKS, ROWS, SL, LANES), F32),
            pltpu.VMEM((CH, SCEN, NB), F32),
            pltpu.VMEM((areas, 8, LANES), F32),
            pltpu.VMEM((areas, 8, LANES), F32),
            pltpu.VMEM((areas, PEER_CAP, 2 * SIDE), F32),
            pltpu.VMEM((areas, PEER_CAP, 2 * SIDE), F32),
            pltpu.VMEM((2, slots, SIDE), F32),
            pltpu.VMEM((NBD, slots), BF16),
            pltpu.VMEM((2, SIDE, NBD), F32),
            dma((12,)),
            dma((NB // BLOCK,)),
            dma((2 * CHUNKS + 2,)),
            dma((CHUNKS, RANKS - 1)),
            dma((CHUNKS, RANKS - 1)),
            dma((CHUNKS, RANKS - 1)),
            dma((CHUNKS, RANKS - 1)),
            dma((areas,)),
            dma((areas,)),
            dma((areas,)),
            dma((areas,)),
            pltpu.SemaphoreType.REGULAR,
            pltpu.SemaphoreType.REGULAR,
        ],
        compiler_params=pltpu.CompilerParams(
            collective_id=0, has_side_effects=True, vmem_limit_bytes=60 << 20
        ),
        name="sweep",
    )(
        dev_count,
        volt.reshape(CH, SCEN, NB),
        inject.reshape(CH, SCEN, NB),
        zinv.reshape(CH, NB, NB),
        dev_bus,
        dev_cond,
        dev_sat,
        tie_area.reshape(1, ties),
        tie_bus,
        tie_far,
        tie_res,
        tie_reac,
        synthesis,
        analysis,
    )
    return out.reshape(2, 1, HL, SCEN, NB)


def solution(mesh):
    in_specs = (
        P(None, "area", "harm", None, None),
        P(None, "area", "harm", None, None),
        P(None, "area", "harm", None, None),
        P("area", None),
        P("area"),
        P("area", None),
        P("area", None),
        P("area", None),
        P("area", None, None),
        P("area", None),
        P("area", None),
        P("area", None),
    )
    out_specs = P(None, "area", "harm", None, None)
    return jax.shard_map(
        per_device, mesh=mesh, in_specs=in_specs, out_specs=out_specs, check_vma=False
    )
```

```python
import functools
import math

import jax
import jax.numpy as jnp
import numpy as np
from jax import lax
from jax.experimental import pallas as pl
from jax.experimental.pallas import tpu as pltpu
from jax.sharding import PartitionSpec as P

NB = 768
NBD = 128
H = 28
TS = 512
HALF = TS // 2
CAP = 2048
SCEN = 32
PEER_CAP = 16
RANKS = 4
HL = H // RANKS
CH = 2 * HL
ROWS = RANKS * CH
SL = SCEN // RANKS
LANES = 128
CHUNKS = NB // LANES
LAST = 1
SPLIT = 8
BLOCK = 256
SIDE = 256

MESH = pl.DeviceIdType.MESH
F32 = jnp.float32
BF16 = jnp.bfloat16


def phase_tables():
    samples = np.arange(HALF)[:, None]
    columns = []
    for rank in range(RANKS):
        orders = 2 * (rank * HL + np.arange(HL))[None, :] + 1
        angles = (samples * orders % TS) * (2.0 * math.pi / TS)
        columns += [np.cos(angles), -np.sin(angles)]
    table = np.concatenate(columns, axis=1)

    def split(values):
        high = values.astype(np.float32).astype(BF16)
        low = (values - high.astype(np.float64)).astype(np.float32).astype(BF16)
        return high, low

    high, low = split(2.0 * table)
    synthesis = np.concatenate([high, high, low], axis=1)
    turned = table.T.reshape(RANKS, 2, HL, HALF).swapaxes(1, 2).reshape(ROWS, HALF)
    high, low = split((4.0 / TS) * turned)
    analysis = np.concatenate([high, low], axis=0)
    return jnp.asarray(synthesis), jnp.asarray(analysis)


def split_two(values):
    high = values.astype(BF16).astype(F32)
    return high, values - high


def dot_rows(left, right):
    return lax.dot_general(
        left, right, (((1,), (1,)), ((), ())), preferred_element_type=F32
    )


def kernel(
    areas,
    ties,
    groups,
    count_h,
    volt_h,
    inject_h,
    zinv_h,
    bus_h,
    cond_h,
    sat_h,
    tarea_h,
    tbus_h,
    tfar_h,
    tres_h,
    treac_h,
    synth_h,
    anal_h,
    out_ref,
    volt_v,
    inject_v,
    zinv_v,
    bus_v,
    cond_v,
    sat_v,
    tarea_v,
    tbus_v,
    tfar_v,
    tres_v,
    treac_v,
    synth_v,
    anal_v,
    fwd_v,
    res_v,
    ret_v,
    req_s,
    req_r,
    tie_s,
    tie_r,
    adm_v,
    place_v,
    tie_v,
    load_sem,
    zinv_sem,
    self_sem,
    fs_sem,
    fr_sem,
    bs_sem,
    br_sem,
    qs_sem,
    qr_sem,
    ts_sem,
    tr_sem,
    entry_sem,
    plane_sem,
    count_s,
    edge_v,
    edge_sem,
):
    slots = areas * PEER_CAP
    area = lax.axis_index("area")
    rank = lax.axis_index("harm")

    barrier = pltpu.get_barrier_semaphore()
    for step in range(1, RANKS):
        pl.semaphore_signal(
            barrier, inc=1, device_id=(area, (rank + step) % RANKS), device_id_type=MESH
        )

    line = areas // groups
    base = area // line * line
    group = area // line
    place = area - base

    def greet(semaphore, sign):
        for step in range(1, line):
            near = place + sign * step

            @pl.when((near >= 0) & (near < line))
            def _():
                pl.semaphore_signal(
                    semaphore, inc=1, device_id=(base + near, rank), device_id_type=MESH
                )

        for step in range(1, groups):
            other = group + sign * step

            @pl.when((other >= 0) & (other < groups))
            def _():
                pl.semaphore_signal(
                    semaphore,
                    inc=1,
                    device_id=(other * line + place, rank),
                    device_id_type=MESH,
                )

    greet(barrier, 1)

    def rank_rows(which):
        return pl.ds(which * CH, CH)

    def scenarios(which):
        return pl.ds(pl.multiple_of(which * SL, SL), SL)

    def lanes(chunk):
        return pl.ds(pl.multiple_of(chunk * LANES, LANES), LANES)

    def own_forward(chunk):
        return pltpu.make_async_copy(
            volt_h.at[:, scenarios(rank), lanes(chunk)],
            fwd_v.at[chunk, rank_rows(rank)],
            self_sem.at[chunk],
        )

    pl.semaphore_wait(barrier, RANKS - 1 + place + group)

    def forward(chunk, step):
        target = (rank + step) % RANKS
        return pltpu.make_async_remote_copy(
            src_ref=volt_h.at[:, scenarios(target), lanes(chunk)],
            dst_ref=fwd_v.at[chunk, rank_rows(rank)],
            send_sem=fs_sem.at[chunk, step - 1],
            recv_sem=fr_sem.at[chunk, step - 1],
            device_id=(area, target),
            device_id_type=MESH,
        )

    def backward(chunk, step, first=0, count=CH, line=None):
        target = (rank + step) % RANKS
        line = chunk if line is None else line
        return pltpu.make_async_remote_copy(
            src_ref=res_v.at[chunk, pl.ds(target * CH + first, count)],
            dst_ref=ret_v.at[pl.ds(first, count), scenarios(rank), lanes(chunk)],
            send_sem=bs_sem.at[line, step - 1],
            recv_sem=br_sem.at[line, step - 1],
            device_id=(area, target),
            device_id_type=MESH,
        )

    def last_part(part, step):
        return backward(
            LAST, step, part * SPLIT, (SPLIT, CH - SPLIT)[part], LAST + part * (CHUNKS - LAST)
        )

    def each_target(action):
        for target in range(RANKS):

            @pl.when(rank != target)
            def _():
                action((target - rank + RANKS) % RANKS)

    def own_backward(chunk):
        return pltpu.make_async_copy(
            res_v.at[chunk, rank_rows(rank)],
            ret_v.at[:, scenarios(rank), lanes(chunk)],
            self_sem.at[CHUNKS + chunk],
        )

    def request(step):
        target = (area + step) % areas
        return pltpu.make_async_remote_copy(
            src_ref=req_s.at[target],
            dst_ref=req_r.at[area],
            send_sem=qs_sem.at[step],
            recv_sem=qr_sem.at[step],
            device_id=(target, rank),
            device_id_type=MESH,
        )

    def answer(step):
        target = (area + step) % areas
        return pltpu.make_async_remote_copy(
            src_ref=tie_s.at[target],
            dst_ref=tie_r.at[area],
            send_sem=ts_sem.at[step],
            recv_sem=tr_sem.at[step],
            device_id=(target, rank),
            device_id_type=MESH,
        )

    def each_area(action):
        def run(step, carry):
            action(step)
            return carry

        lax.fori_loop(1, areas, run, 0)

    def nth(i):
        return (i + 2) % CHUNKS

    def send_forward(i, carry):
        for step in (2, 1, 3):
            forward(nth(i), step).start()
        return carry

    lax.fori_loop(0, CHUNKS, send_forward, 0)
    greet(entry_sem, -1)

    pairs = [
        (tarea_h, tarea_v),
        (tbus_h, tbus_v),
        (tfar_h, tfar_v),
        (tres_h, tres_v),
        (treac_h, treac_v),
        (volt_h, volt_v),
        (bus_h, bus_v),
        (cond_h, cond_v),
        (sat_h, sat_v),
        (synth_h, synth_v),
        (anal_h, anal_v),
        (inject_h, inject_v),
        (count_h, count_s),
    ]
    loads = [
        pltpu.make_async_copy(source, target, load_sem.at[i])
        for i, (source, target) in enumerate(pairs)
    ]
    for load in loads:
        load.start()

    for chunk in range(CHUNKS):
        own_forward(chunk).start()

    order = (1, 2)

    def zinv_copy(block):
        return pltpu.make_async_copy(
            zinv_h.at[:, :, pl.ds(block * BLOCK, BLOCK)],
            zinv_v.at[:, :, pl.ds(block * BLOCK, BLOCK)],
            zinv_sem.at[block],
        )

    def edge_copy(chunk, part):
        return pltpu.make_async_copy(
            zinv_h.at[pl.ds(part * HL, HL), :, pl.ds(chunk * LANES, LANES)],
            edge_v.at[chunk, :, :, pl.ds(part * LANES, LANES)],
            edge_sem.at[chunk, part],
        )

    for block in order:
        zinv_copy(block).start()
    for chunk in range(2):
        for part in range(2):
            edge_copy(chunk, part).start()

    for load in loads[:5]:
        load.wait()
    tie_rows = lax.broadcasted_iota(jnp.int32, (ties, ties), 0)
    tie_cols = lax.broadcasted_iota(jnp.int32, (ties, ties), 1)
    named = jnp.broadcast_to(tarea_v[...], (ties, ties))
    named_column = jnp.sum(
        jnp.where(tie_rows == tie_cols, named, 0), axis=1, keepdims=True
    )
    earlier = jnp.sum(
        jnp.where((named == named_column) & (tie_rows < tie_cols), 1, 0),
        axis=0,
        keepdims=True,
    )
    slot_row = tarea_v[...] * PEER_CAP + earlier
    slot_ids = lax.broadcasted_iota(jnp.int32, (slots, ties), 0)
    placed = jnp.where(slot_row == slot_ids, 1.0, 0.0).astype(BF16)
    bus_ids = lax.broadcasted_iota(jnp.int32, (NBD, ties), 0)
    area_ids = lax.broadcasted_iota(jnp.int32, (areas, ties), 0)
    of_area = jnp.where(tarea_v[...] == area_ids, 1.0, 0.0).astype(BF16)
    wish = (tfar_v[...] + 1).astype(F32)
    of_turn = jnp.where(earlier == bus_ids, wish, 0.0).astype(BF16)
    wishes = dot_rows(of_area, of_turn)
    req_s[...] = jnp.broadcast_to(wishes[:, None, :], (areas, 8, LANES))

    later = line - 1 - place + groups - 1 - group

    @pl.when(later > 0)
    def _():
        pl.semaphore_wait(entry_sem, later)

    for step in range(1, groups):
        peer = (area + step * line) % areas
        pl.semaphore_signal(
            plane_sem, inc=1, device_id=(peer, rank), device_id_type=MESH
        )
    pl.semaphore_wait(plane_sem, groups - 1)
    each_area(lambda step: request(step).start())
    own_request = pltpu.make_async_copy(
        req_s.at[area], req_r.at[area], self_sem.at[2 * CHUNKS]
    )
    own_request.start()

    tie_bus_pick = jnp.where(tbus_v[...] == bus_ids, 1.0, 0.0).astype(BF16)
    place_v[...] = dot_rows(tie_bus_pick, placed).astype(BF16)
    resist_high, resist_low = split_two(tres_v[...])
    react_high, react_low = split_two(treac_v[...])
    row_ids = lax.broadcasted_iota(jnp.int32, (8, ties), 0)
    columns = jnp.where(row_ids == 0, resist_high, jnp.where(row_ids == 1, resist_low, 0.0))
    columns = jnp.where(row_ids == 2, react_high, jnp.where(row_ids == 3, react_low, columns))
    columns = jnp.where(row_ids == 4, 1.0, columns).astype(BF16)
    at_slot = dot_rows(placed, columns)
    resist = at_slot[:, 0:1] + at_slot[:, 1:2] + (1.0 - at_slot[:, 4:5])
    lane_ids = lax.broadcasted_iota(jnp.int32, (1, SIDE), 1)
    orders = (2 * (rank * HL + lane_ids // SCEN) + 1).astype(F32)
    reactance = (at_slot[:, 2:3] + at_slot[:, 3:4]) * orders
    denominator = resist * resist + reactance * reactance
    adm_v[0] = resist / denominator
    adm_v[1] = -reactance / denominator

    for load in loads[6:9] + loads[12:]:
        load.wait()
    totals = jnp.zeros((8, NB), F32)
    row_ids = lax.broadcasted_iota(jnp.int32, (8, BLOCK), 0)
    for part in range(CAP // BLOCK):
        here = slice(part * BLOCK, (part + 1) * BLOCK)
        slot = part * BLOCK + lax.broadcasted_iota(jnp.int32, (1, BLOCK), 1)
        live = jnp.where(slot < count_s[0], 1.0, 0.0)
        rows = []
        for values in (cond_v[:, here], sat_v[:, here]):
            high, rest = split_two(live * values)
            middle, low = split_two(rest)
            rows += [high, middle, low]
        coefficients = jnp.zeros((8, BLOCK), F32)
        for i, row in enumerate(rows):
            coefficients = jnp.where(row_ids == i, row, coefficients)
        bus_rows = lax.broadcasted_iota(jnp.int32, (NB, BLOCK), 0)
        pick = jnp.where(bus_v[:, here] == bus_rows, 1.0, 0.0).astype(BF16)
        totals = totals + dot_rows(coefficients.astype(BF16), pick)
    conductance = totals[0:1] + totals[1:2] + totals[2:3]
    saturation = totals[3:4] + totals[4:5] + totals[5:6]

    for load in loads[9:12]:
        load.wait()
    loads[5].wait()

    def law(i, carry):
        chunk = nth(i)
        own_forward(chunk).wait()
        for step in range(1, RANKS):
            forward(chunk, step).wait_recv()
        for s in range(0, SL, 2):
            pair = jnp.concatenate(
                [
                    fwd_v[chunk, :, s, :],
                    fwd_v[chunk, :, s + 1, :],
                ],
                axis=1,
            )
            high, low = split_two(pair)
            stacked = jnp.concatenate([high, low, high], axis=0).astype(BF16)
            wave = jnp.dot(synth_v[...], stacked, preferred_element_type=F32)
            shape = jnp.tanh(wave).astype(BF16)
            both = jnp.dot(anal_v[...], shape, preferred_element_type=F32)
            harmonics = both[:ROWS] + both[ROWS:]
            res_v[chunk, :, s, :] = harmonics[:, :LANES]
            res_v[chunk, :, s + 1, :] = harmonics[:, LANES:]
        own_backward(chunk).start()

        @pl.when(chunk != LAST)
        def _():
            for step in (1, 3, 2):
                backward(chunk, step).start()

        @pl.when(chunk == LAST)
        def _():
            each_target(lambda step: last_part(0, step).start())
            each_target(lambda step: last_part(1, step).start())

        return carry

    lax.fori_loop(0, 3, law, 0)

    each_area(lambda step: request(step).wait_recv())
    own_request.wait()
    asked = req_r[:, 0, :].astype(BF16)
    slot_rows = lax.broadcasted_iota(jnp.int32, (slots, areas), 0) // PEER_CAP
    slot_cols = lax.broadcasted_iota(jnp.int32, (slots, areas), 1)
    spread = jnp.where(slot_rows == slot_cols, 1.0, 0.0).astype(BF16)
    asked = jnp.dot(spread, asked, preferred_element_type=F32)
    turn_ids = lax.broadcasted_iota(jnp.int32, (slots, LANES), 0) % PEER_CAP
    far_ids = lax.broadcasted_iota(jnp.int32, (slots, LANES), 1)
    asked = jnp.sum(
        jnp.where(turn_ids == far_ids, asked, 0.0), axis=1, keepdims=True
    ).astype(jnp.int32)
    wanted = jnp.where(asked == far_ids + 1, 1.0, 0.0).astype(BF16)
    wanted = jnp.concatenate([wanted, wanted], axis=1)
    for part in range(2):
        edge = volt_v[part * HL : (part + 1) * HL, :, :NBD].reshape(HL * SCEN, NBD)
        high, low = split_two(edge)
        edge = jnp.concatenate([high, low], axis=1).astype(BF16)
        edge = jnp.concatenate(
            [edge, jnp.zeros((SIDE - HL * SCEN, 2 * NBD), BF16)], axis=0
        )
        tie_s[:, :, part * SIDE : (part + 1) * SIDE] = dot_rows(wanted, edge).reshape(
            areas, PEER_CAP, SIDE
        )
    each_area(lambda step: answer(step).start())
    own_answer = pltpu.make_async_copy(
        tie_s.at[area], tie_r.at[area], self_sem.at[2 * CHUNKS + 1]
    )
    own_answer.start()

    lax.fori_loop(3, CHUNKS, law, 0)

    def result_in(chunk):
        own_backward(chunk).wait()
        for step in range(1, RANKS):
            backward(chunk, step).wait_recv()

    def gather_ties():
        each_area(lambda step: answer(step).wait_recv())
        own_answer.wait()
        far = tie_r[...].reshape(slots, 2 * SIDE)
        far_real, far_imag = far[:, :SIDE], far[:, SIDE:]
        adm_real, adm_imag = adm_v[0], adm_v[1]
        for part, value in enumerate(
            (
                adm_real * far_real - adm_imag * far_imag,
                adm_real * far_imag + adm_imag * far_real,
            )
        ):
            high, low = split_two(value)
            summed = jnp.dot(
                place_v[...], high.astype(BF16), preferred_element_type=F32
            ) + jnp.dot(place_v[...], low.astype(BF16), preferred_element_type=F32)
            tie_v[part] = summed.T

    def accumulate(first, chunks, fresh, low=0, high=HL):
        here = slice(first * LANES, (first + chunks) * LANES)
        for h in range(low, high):
            sides = []
            for part in range(2):
                row = part * HL + h
                value = (
                    inject_v[row, :, here]
                    + conductance[:, here] * volt_v[row, :, here]
                    + saturation[:, here] * ret_v[2 * h + part, :, here]
                )
                if first == 0:
                    value = value + tie_v[part, h * SCEN : (h + 1) * SCEN, :]
                sides.append(value)
            real, imag = sides
            straight = jnp.concatenate([real, imag], axis=0).astype(BF16)
            turned = jnp.concatenate([-imag, real], axis=0).astype(BF16)
            if chunks == 1:
                total = dot_rows(
                    jnp.concatenate([straight, turned], axis=1), edge_v[first, h]
                )
            else:
                total = dot_rows(straight, zinv_v[h, :, here]) + dot_rows(
                    turned, zinv_v[HL + h, :, here]
                )
            if fresh:
                out_ref[h] = total[:SCEN]
                out_ref[HL + h] = total[SCEN:]
            else:
                out_ref[h] += total[:SCEN]
                out_ref[HL + h] += total[SCEN:]

    for turn, block in enumerate(order):
        if turn == 1:
            gather_ties()
        zinv_copy(block).wait()
        result_in(2 * block)
        result_in(2 * block + 1)
        accumulate(2 * block, 2, turn == 0)
    for chunk in range(2):
        for part in range(2):
            edge_copy(chunk, part).wait()
    result_in(0)
    accumulate(0, 1, False)
    own_backward(LAST).wait()
    for part in range(2):
        for step in range(1, RANKS):
            last_part(part, step).wait_recv()
        middle = SPLIT // 2
        accumulate(LAST, 1, False, *((0, middle), (middle, HL))[part])

    def drain(i, carry):
        for step in range(1, RANKS):
            forward(i, step).wait_send()

            @pl.when(i != LAST)
            def _():
                backward(i, step).wait_send()

        return carry

    lax.fori_loop(0, CHUNKS, drain, 0)
    for part in range(2):
        for step in range(1, RANKS):
            last_part(part, step).wait_send()
    each_area(lambda step: request(step).wait_send())
    each_area(lambda step: answer(step).wait_send())


def per_device(
    volt,
    inject,
    zinv,
    dev_bus,
    dev_count,
    dev_cond,
    dev_sat,
    tie_bus,
    tie_area,
    tie_far,
    tie_res,
    tie_reac,
):
    areas = lax.axis_size("area")
    ties = tie_bus.shape[1]
    slots = areas * PEER_CAP
    synthesis, analysis = phase_tables()
    anywhere = pl.BlockSpec(memory_space=pl.ANY)
    dma = pltpu.SemaphoreType.DMA
    out = pl.pallas_call(
        functools.partial(kernel, areas, ties, 4 if areas > 8 else 2),
        out_shape=pltpu.VMEM((CH, SCEN, NB), F32),
        in_specs=[anywhere] * 14,
        out_specs=pl.BlockSpec(memory_space=pltpu.VMEM),
        scratch_shapes=[
            pltpu.VMEM((CH, SCEN, NB), F32),
            pltpu.VMEM((CH, SCEN, NB), F32),
            pltpu.VMEM((CH, NB, NB), BF16),
            pltpu.VMEM((1, CAP), jnp.int32),
            pltpu.VMEM((1, CAP), F32),
            pltpu.VMEM((1, CAP), F32),
            pltpu.VMEM((1, ties), jnp.int32),
            pltpu.VMEM((1, ties), jnp.int32),
            pltpu.VMEM((1, ties), jnp.int32),
            pltpu.VMEM((1, ties), F32),
            pltpu.VMEM((1, ties), F32),
            pltpu.VMEM(synthesis.shape, BF16),
            pltpu.VMEM(analysis.shape, BF16),
            pltpu.VMEM((CHUNKS, ROWS, SL, LANES), F32),
            pltpu.VMEM((CHUNKS, ROWS, SL, LANES), F32),
            pltpu.VMEM((CH, SCEN, NB), F32),
            pltpu.VMEM((areas, 8, LANES), F32),
            pltpu.VMEM((areas, 8, LANES), F32),
            pltpu.VMEM((areas, PEER_CAP, 2 * SIDE), F32),
            pltpu.VMEM((areas, PEER_CAP, 2 * SIDE), F32),
            pltpu.VMEM((2, slots, SIDE), F32),
            pltpu.VMEM((NBD, slots), BF16),
            pltpu.VMEM((2, SIDE, NBD), F32),
            dma((13,)),
            dma((NB // BLOCK,)),
            dma((2 * CHUNKS + 2,)),
            dma((CHUNKS, RANKS - 1)),
            dma((CHUNKS, RANKS - 1)),
            dma((CHUNKS + 1, RANKS - 1)),
            dma((CHUNKS + 1, RANKS - 1)),
            dma((areas,)),
            dma((areas,)),
            dma((areas,)),
            dma((areas,)),
            pltpu.SemaphoreType.REGULAR,
            pltpu.SemaphoreType.REGULAR,
            pltpu.SMEM((1,), jnp.int32),
            pltpu.VMEM((2, HL, NB, 2 * LANES), BF16),
            dma((2, 2)),
        ],
        compiler_params=pltpu.CompilerParams(
            collective_id=0, has_side_effects=True, vmem_limit_bytes=60 << 20
        ),
        name="sweep",
    )(
        dev_count,
        volt.reshape(CH, SCEN, NB),
        inject.reshape(CH, SCEN, NB),
        zinv.reshape(CH, NB, NB),
        dev_bus,
        dev_cond,
        dev_sat,
        tie_area.reshape(1, ties),
        tie_bus,
        tie_far,
        tie_res,
        tie_reac,
        synthesis,
        analysis,
    )
    return out.reshape(2, 1, HL, SCEN, NB)


def solution(mesh):
    in_specs = (
        P(None, "area", "harm", None, None),
        P(None, "area", "harm", None, None),
        P(None, "area", "harm", None, None),
        P("area", None),
        P("area"),
        P("area", None),
        P("area", None),
        P("area", None),
        P("area", None, None),
        P("area", None),
        P("area", None),
        P("area", None),
    )
    out_specs = P(None, "area", "harm", None, None)
    return jax.shard_map(
        per_device, mesh=mesh, in_specs=in_specs, out_specs=out_specs, check_vma=False
    )
```
